32 devices in a mesh: groups: 2 (over y), ctx: 4 (over x, core), head: 4 (over z).
Axes of the slice: x: 2, y: 2, z: 4, core: 2. Of those that a mesh axis runs over, the one named last changes fastest.
Arguments:
- tokens_in: bfloat16 [8192, 4096], P(('groups', 'ctx')), parts along dimension 0, may hold values from -16 to 16
- tempo_ids: int32 [8192], P(('groups', 'ctx')), parts along dimension 0, may hold values from 0 to 63
- tempo_table: bfloat16 [64, 4096], replicated, may hold values from -6 to 6
- w_query: bfloat16 [4096, 2048], P('ctx', 'head'), may hold values from -0.1875 to 0.1875
- w_key: bfloat16 [4096, 2048], P('ctx', 'head'), may hold values from -0.09375 to 0.09375
- w_value: bfloat16 [4096, 2048], P('ctx', 'head'), may hold values from -0.09375 to 0.09375
Outputs:
- attended: bfloat16 [8192, 2048], P(('groups', 'ctx'), 'head'), parts along dimension 0
The draws below stay inside these ranges and needn't reach their ends.
There are 2 independent parts, one for each index of `groups`. The reference program is written for one: setup_inputs(seed, part) draws one part's arguments, and reference() takes and returns one part's arrays. A program takes and returns all parts, laid end to end along the dimension named above; an argument that names none is the same for every part. Nothing has to cross between parts.
All inputs are finite; a program needn't handle non-finite values.
Results may differ from the reference program's by a relative error of at most 0.029.
Values may be sent and summed in bfloat16 or wider, within the bound.
No kernel may reach another device: no remote copies, remote signals or barrier semaphores. Data moves between devices by JAX's collectives and lax.ppermute only.
A program may use at most 64 MiB of HBM per device.

```python
import jax
import jax.numpy as jnp
from jax import lax

D = 4096
HEAD_DIM = 128
HEADS = 16
TEMPOS = 64
SPAN = 1024
BEACONS = 32
POOL = 32
TOKENS = 4096


def draw_tokens_in(key, part):
    first = jax.random.fold_in(key, 0)
    base = jnp.clip(jax.random.normal(first, (TOKENS, D), jnp.float32), -6.0, 6.0)
    return base.astype(jnp.bfloat16)


def touch_ends(result, stream_key, low, high):
    spot = [jax.random.randint(jax.random.fold_in(stream_key, axis), (), 0, length) for axis, length in enumerate(result.shape)]
    main_axis = result.shape.index(max(result.shape))
    neighbour = spot[:main_axis] + [(spot[main_axis] + 1) % result.shape[main_axis]] + spot[main_axis + 1:]
    return result.at[tuple(spot)].set(low).at[tuple(neighbour)].set(high)


def block_levels(key, shape, pieces, least, top_value):
    loudness = 1.0
    for dim, shards_of in pieces:
        draws = jax.random.uniform(jax.random.fold_in(jax.random.fold_in(key, 6), dim), (shards_of,), jnp.float32, least / len(pieces), top_value / len(pieces))
        loudness = loudness * jnp.repeat(jnp.exp(draws), shape[dim] // shards_of).reshape((-1,) + (1,) * (len(shape) - 1 - dim))
    return loudness


def bell_draw(own_key, extent, spread, reach, cuts=(), held_as=jnp.bfloat16):
    result = spread * jax.random.normal(own_key, extent, jnp.float32)
    if cuts:
        result = result * block_levels(own_key, extent, cuts, -0.22, 0.18)
    return jnp.clip(result, -reach, reach).astype(held_as)


def setup_inputs(seed: int = 0, part: int = 0) -> dict:
    arg_keys = jax.random.split(jax.random.key(seed), 7)
    part_splits = jax.random.split(jax.random.fold_in(arg_keys[6], part), 7)
    return {
        "tokens_in": draw_tokens_in(jax.random.fold_in(jax.random.fold_in(arg_keys[6], part), 71), part),
        "tempo_ids": touch_ends(jax.random.randint(part_splits[1], (TOKENS,), 0, TEMPOS), jax.random.fold_in(part_splits[1], 1), 0, TEMPOS - 1).astype(jnp.int32),
        "tempo_table": bell_draw(arg_keys[2], (TEMPOS, D), 1.0, 6.0),
        "w_query": bell_draw(arg_keys[3], (D, HEADS * HEAD_DIM), (D // 4) ** -0.5, 0.1875, ((0, 4), (1, 4))),
        "w_key": bell_draw(arg_keys[4], (D, HEADS * HEAD_DIM), D ** -0.5, 0.09375, ((0, 4), (1, 4))),
        "w_value": bell_draw(arg_keys[5], (D, HEADS * HEAD_DIM), D ** -0.5, 0.09375, ((0, 4), (1, 4))),
    }


LOWEST = -1.0e30


def reference(tokens_in, tempo_ids, tempo_table, w_query, w_key, w_value):
    width_all = HEADS * HEAD_DIM
    selector = (tempo_ids[:, None] == jnp.arange(TEMPOS, dtype=jnp.int32)[None, :]).astype(tempo_table.dtype)
    hidden = (tokens_in.astype(jnp.float32) + jnp.dot(selector, tempo_table, preferred_element_type=jnp.float32)).astype(jnp.bfloat16)
    queries = jnp.dot(hidden, w_query, preferred_element_type=jnp.float32).astype(jnp.bfloat16)
    keys = jnp.dot(hidden, w_key, preferred_element_type=jnp.float32).astype(jnp.bfloat16)
    values = jnp.dot(hidden, w_value, preferred_element_type=jnp.float32).astype(jnp.bfloat16)
    span_count = TOKENS // SPAN
    slot_count = span_count * BEACONS
    beacon_keys = (jnp.sum(keys.reshape(slot_count, POOL, width_all).astype(jnp.float32), axis=1) * POOL ** -0.5).astype(jnp.bfloat16)
    beacon_values = (jnp.sum(values.reshape(slot_count, POOL, width_all).astype(jnp.float32), axis=1) * POOL ** -0.5).astype(jnp.bfloat16)
    slot_span = jnp.arange(slot_count, dtype=jnp.int32) // BEACONS
    causal = jnp.arange(SPAN, dtype=jnp.int32)[:, None] >= jnp.arange(SPAN, dtype=jnp.int32)[None, :]

    def one_span(index):
        start = index * SPAN
        span_queries = lax.dynamic_slice_in_dim(queries, start, SPAN, 0).reshape(SPAN, HEADS, HEAD_DIM).astype(jnp.float32)
        span_keys = lax.dynamic_slice_in_dim(keys, start, SPAN, 0).reshape(SPAN, HEADS, HEAD_DIM)
        span_values = lax.dynamic_slice_in_dim(values, start, SPAN, 0).reshape(SPAN, HEADS, HEAD_DIM)
        all_keys = jnp.concatenate([beacon_keys.reshape(slot_count, HEADS, HEAD_DIM), span_keys], axis=0).astype(jnp.float32)
        all_values = jnp.concatenate([beacon_values.reshape(slot_count, HEADS, HEAD_DIM), span_values], axis=0).astype(jnp.float32)
        earlier = jnp.broadcast_to((slot_span < index)[None, :], (SPAN, slot_count))
        allowed = jnp.concatenate([earlier, causal], axis=1)[None]
        scores = jnp.einsum("qhd,khd->hqk", span_queries, all_keys) * (HEAD_DIM ** -0.5)
        masked = jnp.where(allowed, scores, LOWEST)
        highest = jnp.max(masked, axis=2, keepdims=True)
        weights = jnp.where(allowed, jnp.exp(masked - highest), 0.0)
        totals = jnp.sum(weights, axis=2)
        rounded = lax.optimization_barrier(weights.astype(jnp.bfloat16))
        summed = jnp.einsum("hqk,khd->qhd", rounded.astype(jnp.float32), all_values)
        return (summed / totals.T[:, :, None]).reshape(SPAN, width_all).astype(jnp.bfloat16)

    outputs = lax.map(one_span, jnp.arange(span_count, dtype=jnp.int32))
    return outputs.reshape(TOKENS, width_all)
```

```python
import functools

import jax
import jax.numpy as jnp
from jax import lax
from jax.experimental import pallas as pl
from jax.experimental.pallas import tpu as pltpu
from jax.sharding import PartitionSpec as P

HEAD_DIM = 128
SPAN = 1024
BEACONS = 32
POOL = 32


LOWEST = -1e30
LOG2_E = 1.4426950408889634
TILE = 256


def by_heads(matrix, heads_local):
    return matrix.reshape(matrix.shape[0], heads_local, -1).transpose(1, 0, 2)


def partial_attend(queries, keys, values, allowed):
    scores = jnp.einsum(
        "hqd,hkd->hqk", queries, keys, preferred_element_type=jnp.float32
    ) * queries.shape[-1] ** (-0.5)
    masked = jnp.where(allowed, scores, LOWEST)
    highest = jnp.max(masked, axis=2)
    weights = jnp.where(allowed, jnp.exp(masked - highest[..., None]), 0.0)
    totals = jnp.sum(weights, axis=2)
    summed = jnp.einsum(
        "hqk,hkd->hqd", weights.astype(jnp.bfloat16), values, preferred_element_type=jnp.float32
    )
    return (highest, totals, summed)


def combine_partials(first, second):
    highest = jnp.maximum(first[0], second[0])
    left_factor = jnp.exp(first[0] - highest)
    right_factor = jnp.exp(second[0] - highest)
    totals = first[1] * left_factor + second[1] * right_factor
    summed = first[2] * left_factor[..., None] + second[2] * right_factor[..., None]
    return (highest, totals, summed)


def beacon_partial(
    queries, query_span, beacon_keys, beacon_values, low_rank, high_rank, group, slots_dev
):
    heads_local, query_count, head_size = queries.shape
    block_width = group * slots_dev
    start_state = (
        jnp.full((heads_local, query_count), LOWEST, jnp.float32),
        jnp.zeros((heads_local, query_count), jnp.float32),
        jnp.zeros((heads_local, query_count, head_size), jnp.float32),
    )

    def visit(block, state):
        first_slot = block * block_width
        block_keys = lax.dynamic_slice_in_dim(beacon_keys, first_slot, block_width, 1)
        block_values = lax.dynamic_slice_in_dim(beacon_values, first_slot, block_width, 1)
        slot_index = first_slot + jnp.arange(block_width, dtype=jnp.int32)
        owner = slot_index // slots_dev
        in_range = (owner >= low_rank) & (owner < high_rank)
        earlier = (slot_index // BEACONS)[None, :] < query_span[:, None]
        allowed = (in_range[None, :] & earlier)[None]
        return combine_partials(state, partial_attend(queries, block_keys, block_values, allowed))

    first_block = low_rank // group
    last_block = (high_rank + group - 1) // group
    return lax.fori_loop(first_block, last_block, visit, start_state)


def on_device_general(tokens_in, tempo_ids, tempo_table, w_query, w_key, w_value):
    row_count = tokens_in.shape[0]
    col_width = w_query.shape[1]
    heads_local = col_width // HEAD_DIM
    ctx_count = lax.axis_size("ctx")
    ctx_rank = lax.axis_index("ctx")
    spans_dev = row_count // SPAN
    slots_dev = spans_dev * BEACONS
    target = max(1, 256 // slots_dev)
    group = min(ctx_count, 1 << target.bit_length() - 1)
    selector = (
        tempo_ids[:, None] == jnp.arange(tempo_table.shape[0], dtype=jnp.int32)[None, :]
    ).astype(jnp.bfloat16)
    hidden = (
        tokens_in.astype(jnp.float32)
        + jnp.dot(selector, tempo_table, preferred_element_type=jnp.float32)
    ).astype(jnp.bfloat16)
    pieces = (
        lax.all_gather(w_query, "ctx", axis=0, tiled=True),
        lax.all_gather(w_key, "ctx", axis=0, tiled=True),
        lax.all_gather(w_value, "ctx", axis=0, tiled=True),
    )
    projected = tuple(
        (jnp.dot(hidden, piece, preferred_element_type=jnp.float32) for piece in pieces)
    )
    queries = projected[0].astype(jnp.bfloat16)
    keys = projected[1].astype(jnp.bfloat16)
    values = projected[2].astype(jnp.bfloat16)
    pool_scale = POOL ** (-0.5)
    own_keys = (
        jnp.sum(keys.reshape(slots_dev, POOL, col_width).astype(jnp.float32), axis=1) * pool_scale
    ).astype(jnp.bfloat16)
    own_values = (
        jnp.sum(values.reshape(slots_dev, POOL, col_width).astype(jnp.float32), axis=1) * pool_scale
    ).astype(jnp.bfloat16)
    every_keys, every_values = (
        lax.all_gather(own_keys, "ctx", axis=0, tiled=True),
        lax.all_gather(own_values, "ctx", axis=0, tiled=True),
    )
    beacon_keys = by_heads(every_keys, heads_local)
    beacon_values = by_heads(every_values, heads_local)
    query_heads = by_heads(queries, heads_local)
    local_span = jnp.arange(row_count, dtype=jnp.int32) // SPAN
    own_span = ctx_rank * spans_dev + local_span

    def fold_spans(matrix):
        return by_heads(matrix, heads_local)

    causal = (
        jnp.arange(SPAN, dtype=jnp.int32)[:, None] >= jnp.arange(SPAN, dtype=jnp.int32)[None, :]
    )[None]
    inside = partial_attend(fold_spans(queries), fold_spans(keys), fold_spans(values), causal)
    inside = (inside[0], inside[1], inside[2])
    upper_rank = ctx_rank + 1
    remote = beacon_partial(
        query_heads,
        own_span,
        beacon_keys,
        beacon_values,
        jnp.zeros((), jnp.int32),
        upper_rank,
        group,
        slots_dev,
    )
    highest, totals, summed = combine_partials(inside, remote)
    attended = summed / totals[..., None]
    return attended.transpose(1, 0, 2).reshape(row_count, col_width).astype(jnp.bfloat16)


def mm(a, b):
    return jnp.dot(a, b, preferred_element_type=jnp.float32)


def cost(flops, moved, exps=0):
    return pl.CostEstimate(flops=flops, bytes_accessed=moved, transcendentals=exps)


def hidden_kernel(ids_ref, tokens_ref, table_ref, out_ref):
    buckets, width = table_ref.shape
    rows = tokens_ref.shape[0]
    bucket = lax.broadcasted_iota(jnp.int32, (buckets, rows), 0)
    picked = jnp.where(bucket == ids_ref[...], 1.0, 0.0).astype(jnp.bfloat16)
    step = min(width, 512)
    for col in range(0, width, step):
        tempo = lax.dot_general(
            picked,
            table_ref[:, col : col + step],
            (((0,), (0,)), ((), ())),
            preferred_element_type=jnp.float32,
        )
        tokens = tokens_ref[:, col : col + step].astype(jnp.float32)
        out_ref[:, col : col + step] = (tokens + tempo).astype(out_ref.dtype)


def make_hidden(tokens_in, tempo_ids, tempo_table):
    rows, width = tokens_in.shape
    buckets = tempo_table.shape[0]
    return pl.pallas_call(
        hidden_kernel,
        grid=(rows // TILE,),
        in_specs=[
            pl.BlockSpec((1, TILE), lambda i: (0, i)),
            pl.BlockSpec((TILE, width), lambda i: (i, 0)),
            pl.BlockSpec((buckets, width), lambda i: (0, 0)),
        ],
        out_specs=pl.BlockSpec((TILE, width), lambda i: (i, 0)),
        out_shape=jax.ShapeDtypeStruct((rows, width), jnp.bfloat16),
        cost_estimate=cost(2 * rows * 256 * width, 4 * rows * width),
        name="hidden",
    )(tempo_ids.reshape(1, rows), tokens_in, tempo_table)


def local_kernel(s_ref, own_ref, mate_ref, wk_ref, wv_ref, wq_ref, mate_w_ref, out_ref):
    half = wk_ref.shape[1]
    own, mate = own_ref[...], mate_ref[...]
    for place, w_ref in enumerate((wk_ref, wv_ref, wq_ref)):
        out_ref[:, place * half : (place + 1) * half] = mm(own, w_ref[...]) + mm(
            mate, mate_w_ref[place]
        )


def local_part(where, hidden, w_key, w_value, w_query, mate_w):
    rows = hidden.shape[0]
    depth, half = mate_w.shape[1:]
    weight = pl.BlockSpec((depth, half), lambda i, s: (0, lax.rem(s[0], 2)))
    return pl.pallas_call(
        local_kernel,
        grid_spec=pltpu.PrefetchScalarGridSpec(
            num_scalar_prefetch=1,
            grid=(rows // TILE,),
            in_specs=[
                pl.BlockSpec((TILE, depth), lambda i, s: (i, s[0])),
                pl.BlockSpec((TILE, depth), lambda i, s: (i, s[1])),
                weight,
                weight,
                weight,
                pl.BlockSpec((3, depth, half), lambda i, s: (0, 0, 0)),
            ],
            out_specs=pl.BlockSpec((TILE, 3 * half), lambda i, s: (i, 0)),
        ),
        out_shape=jax.ShapeDtypeStruct((rows, 3 * half), jnp.float32),
        cost_estimate=cost(12 * rows * depth * half, 4 * rows * depth + 12 * rows * half),
        name="local_part",
    )(where, hidden, hidden, w_key, w_value, w_query, mate_w)


def key_value_kernel(s_ref, *refs):
    own, mate, sums, weights = refs[0:4], refs[4:8], refs[8:10], refs[10:14]
    keys_ref, values_ref, beacons_ref = refs[14:]
    half = keys_ref.shape[1]

    def finish(hidden, sum_ref):
        for place, out_ref in enumerate((keys_ref, values_ref)):
            total = sum_ref[:, place * half : (place + 1) * half]
            for h_ref, w_ref in zip(hidden, weights):
                total += mm(h_ref[...], w_ref[place])
            rounded = total.astype(jnp.bfloat16)
            out_ref[...] = rounded
            pooled = jnp.sum(
                rounded.astype(jnp.float32).reshape(TILE // POOL, POOL, half), axis=1
            )
            beacons_ref[place] = (pooled * POOL ** (-0.5)).astype(jnp.bfloat16)

    @pl.when(pl.program_id(0) == 0)
    def _():
        finish(own, sums[0])

    @pl.when(pl.program_id(0) == 1)
    def _():
        finish(mate, sums[1])


def keys_values(where, own, mate, own_sum, mate_sum, pieces):
    rows = own.shape[0]
    _, piece, half = pieces[0].shape
    steps = rows // TILE
    pooled = TILE // POOL
    columns = (
        lambda s: 2 * s[2] + s[4],
        lambda s: 2 * s[2] + 1 - s[4],
        lambda s: 2 * s[3] + s[4],
        lambda s: 2 * s[3] + 1 - s[4],
    )
    first = lambda t, i: jnp.where(t == 0, i, steps - 1)
    second = lambda t, i: jnp.where(t == 0, 0, i)

    def block(row, column):
        return pl.BlockSpec((TILE, piece), lambda t, i, s: (row(t, i), column(s)))

    return pl.pallas_call(
        key_value_kernel,
        grid_spec=pltpu.PrefetchScalarGridSpec(
            num_scalar_prefetch=1,
            grid=(2, steps),
            in_specs=[block(first, column) for column in columns]
            + [block(second, column) for column in columns]
            + [
                pl.BlockSpec((TILE, 2 * half), lambda t, i, s: (first(t, i), 0)),
                pl.BlockSpec((TILE, 2 * half), lambda t, i, s: (second(t, i), 0)),
            ]
            + [pl.BlockSpec((2, piece, half), lambda t, i, s: (0, 0, 0))] * 4,
            out_specs=[
                pl.BlockSpec((TILE, half), lambda t, i, s: (t * steps + i, 0)),
                pl.BlockSpec((TILE, half), lambda t, i, s: (t * steps + i, 0)),
                pl.BlockSpec((2, pooled, half), lambda t, i, s: (0, t * steps + i, 0)),
            ],
        ),
        out_shape=[
            jax.ShapeDtypeStruct((2 * rows, half), jnp.bfloat16),
            jax.ShapeDtypeStruct((2 * rows, half), jnp.bfloat16),
            jax.ShapeDtypeStruct((2, 2 * rows // POOL, half), jnp.bfloat16),
        ],
        cost_estimate=cost(
            2 * 2 * rows * 4 * piece * 2 * half, 2 * rows * (8 * piece + 12 * half)
        ),
        name="keys_values",
    )(where, *([own] * 4), *([mate] * 4), own_sum, mate_sum, *pieces)


def attend_kernel(
    turn,
    s_ref,
    h0_ref,
    h1_ref,
    h2_ref,
    sum_ref,
    w0_ref,
    w1_ref,
    w2_ref,
    keys_ref,
    values_ref,
    near_ref,
    far_ref,
    out_ref,
):
    total = sum_ref[...]
    for h_ref, w_ref in ((h0_ref, w0_ref), (h1_ref, w1_ref), (h2_ref, w2_ref)):
        total += mm(h_ref[...], w_ref[...])
    queries = total.astype(jnp.bfloat16)
    half = out_ref.shape[1]
    span = s_ref[turn]
    factor = HEAD_DIM ** (-0.5) * LOG2_E
    contract = (((1,), (1,)), ((), ()))
    slots = near_ref.shape[1] + far_ref.shape[1]
    owner = lax.broadcasted_iota(jnp.int32, (1, slots), 1) // BEACONS
    allowed = jnp.zeros((1, slots), jnp.int32)
    for place in range(slots // BEACONS):
        visible = (s_ref[place] < span).astype(jnp.int32)
        allowed = jnp.where(owner == place, visible, allowed)
    allowed = allowed > 0
    causal = lax.broadcasted_iota(jnp.int32, (TILE, TILE), 0) >= lax.broadcasted_iota(
        jnp.int32, (TILE, TILE), 1
    )
    beacons = jnp.concatenate([near_ref[...], far_ref[...]], axis=1)

    def attend(earlier):
        for low in range(0, half, HEAD_DIM):
            cols = slice(low, low + HEAD_DIM)
            query = queries[:, cols]

            def dots(keys):
                return lax.dot_general(query, keys, contract, preferred_element_type=jnp.float32)

            parts = [
                (
                    jnp.where(allowed, dots(beacons[0, :, cols]), LOWEST),
                    beacons[1, :, cols],
                ),
                (
                    jnp.where(causal, dots(keys_ref[earlier : earlier + TILE, cols]), LOWEST),
                    values_ref[earlier : earlier + TILE, cols],
                ),
            ]
            if earlier:
                parts.append((dots(keys_ref[:earlier, cols]), values_ref[:earlier, cols]))
            highest = functools.reduce(
                jnp.maximum, [jnp.max(score, axis=1, keepdims=True) for score, _ in parts]
            )
            amount = jnp.zeros((TILE, 1), jnp.float32)
            summed = jnp.zeros((TILE, HEAD_DIM), jnp.float32)
            for score, values in parts:
                weights = jnp.exp2((score - highest) * factor)
                amount += jnp.sum(weights, axis=1, keepdims=True)
                summed += mm(weights.astype(jnp.bfloat16), values)
            out_ref[:, cols] = (summed / amount).astype(out_ref.dtype)

    for step in range(SPAN // TILE):

        @pl.when(pl.program_id(0) == step)
        def _():
            attend(step * TILE)


def attend(turn, where, hidden, sums, pieces, keys, values, near, far):
    rows = hidden.shape[0]
    piece, half = pieces[0].shape
    slots = near.shape[1]
    whole = lambda i, s: (0, 0)
    return pl.pallas_call(
        functools.partial(attend_kernel, turn),
        grid_spec=pltpu.PrefetchScalarGridSpec(
            num_scalar_prefetch=1,
            grid=(rows // TILE,),
            in_specs=[
                pl.BlockSpec((TILE, piece), lambda i, s: (i, 2 * s[2] + s[4])),
                pl.BlockSpec((TILE, piece), lambda i, s: (i, 2 * s[2] + 1 - s[4])),
                pl.BlockSpec((TILE, 2 * piece), lambda i, s: (i, s[3])),
                pl.BlockSpec((TILE, half), lambda i, s: (i, 2)),
                pl.BlockSpec((piece, half), whole),
                pl.BlockSpec((piece, half), whole),
                pl.BlockSpec((2 * piece, half), whole),
                pl.BlockSpec((rows, half), lambda i, s: (turn, 0)),
                pl.BlockSpec((rows, half), lambda i, s: (turn, 0)),
                pl.BlockSpec((2, slots, half), lambda i, s: (0, 0, 0)),
                pl.BlockSpec((2, slots, half), lambda i, s: (0, 0, 0)),
            ],
            out_specs=pl.BlockSpec((TILE, half), lambda i, s: (i, 0)),
        ),
        out_shape=jax.ShapeDtypeStruct((rows, half), jnp.bfloat16),
        cost_estimate=cost(
            2 * rows * half * (4 * piece + rows * 2), 8 * rows * piece, rows * rows * 2
        ),
        name="attend_%d" % turn,
    )(where, hidden, hidden, hidden, sums, *pieces, keys, values, near, far)


def on_device(tokens_in, tempo_ids, tempo_table, w_query, w_key, w_value):
    depth, width = w_key.shape
    half = width // 2
    piece = depth // 2
    rank = lax.axis_index("ctx")
    song = lax.axis_index("groups")
    core = rank % 2
    ranks = range(lax.axis_size("ctx"))
    place = lax.iota(jnp.int32, 8)
    where = jnp.where(place == 4, song, rank ^ place)

    def to_mate(array):
        return lax.ppermute(array, "ctx", [(r, r ^ 1) for r in ranks])

    def to_far(array):
        return lax.ppermute(array, "ctx", [(r, r ^ 2) for r in ranks])

    def to_twin(array):
        return lax.ppermute(array, "groups", [(0, 1), (1, 0)])

    def cut(matrix, first, count, side):
        return lax.dynamic_slice(matrix, (first, side * half), (count, half))

    first_row = song * piece
    kv_same_mine = to_far(
        jnp.stack([cut(w, first_row, piece, core) for w in (w_key, w_value)])
    )
    mate_w = to_mate(
        jnp.stack([cut(w, 0, depth, 1 - core) for w in (w_key, w_value, w_query)])
    )
    kv_cross_mine = to_far(lax.dynamic_slice(mate_w, (0, first_row, 0), (2, piece, half)))
    q_same_mine = to_far(cut(w_query, first_row, piece, core))
    q_cross = to_far(mate_w[2])
    kv_same_twin = to_twin(kv_same_mine)
    kv_cross_twin = to_twin(kv_cross_mine)
    q_same_twin = to_twin(q_same_mine)

    own = make_hidden(tokens_in, tempo_ids, tempo_table)
    mate = to_mate(own)
    own_sum = local_part(where, own, w_key, w_value, w_query, mate_w)
    mate_sum = local_part(where, mate, w_key, w_value, w_query, mate_w)
    keys, values, near = keys_values(
        where, own, mate, own_sum, mate_sum, (kv_same_mine, kv_same_twin, kv_cross_mine, kv_cross_twin)
    )
    far = to_far(near)
    q_pieces = (q_same_mine, q_same_twin, q_cross)
    for_mate = attend(1, where, mate, mate_sum, q_pieces, keys, values, near, far)
    from_mate = to_mate(for_mate)
    mine = attend(0, where, own, own_sum, q_pieces, keys, values, near, far)
    return jnp.where(
        core == 0,
        jnp.concatenate([mine, from_mate], axis=1),
        jnp.concatenate([from_mate, mine], axis=1),
    )


def fits(mesh):
    return mesh.shape["ctx"] == 4 and mesh.shape["groups"] == 2


def solution(mesh):
    in_specs = (
        P(("groups", "ctx"), None),
        P(("groups", "ctx")),
        P(),
        P("ctx", "head"),
        P("ctx", "head"),
        P("ctx", "head"),
    )
    out_specs = P(("groups", "ctx"), "head")

    def body(*arrays):
        rows = arrays[0].shape[0]
        even = arrays[3].shape[1] % (2 * HEAD_DIM) == 0
        planned = fits(mesh) and rows == SPAN and even
        return (on_device if planned else on_device_general)(*arrays)

    return jax.shard_map(
        body, mesh=mesh, in_specs=in_specs, out_specs=out_specs, check_vma=False
    )
```

```python
import functools

import jax
import jax.numpy as jnp
from jax import lax
from jax.experimental import pallas as pl
from jax.experimental.pallas import tpu as pltpu
from jax.sharding import PartitionSpec as P

HEAD_DIM = 128
SPAN = 1024
BEACONS = 32
POOL = 32


LOWEST = -1e30
LOG2_E = 1.4426950408889634
TILE = 256


def by_heads(matrix, heads_local):
    return matrix.reshape(matrix.shape[0], heads_local, -1).transpose(1, 0, 2)


def partial_attend(queries, keys, values, allowed):
    scores = jnp.einsum(
        "hqd,hkd->hqk", queries, keys, preferred_element_type=jnp.float32
    ) * queries.shape[-1] ** (-0.5)
    masked = jnp.where(allowed, scores, LOWEST)
    highest = jnp.max(masked, axis=2)
    weights = jnp.where(allowed, jnp.exp(masked - highest[..., None]), 0.0)
    totals = jnp.sum(weights, axis=2)
    summed = jnp.einsum(
        "hqk,hkd->hqd", weights.astype(jnp.bfloat16), values, preferred_element_type=jnp.float32
    )
    return (highest, totals, summed)


def combine_partials(first, second):
    highest = jnp.maximum(first[0], second[0])
    left_factor = jnp.exp(first[0] - highest)
    right_factor = jnp.exp(second[0] - highest)
    totals = first[1] * left_factor + second[1] * right_factor
    summed = first[2] * left_factor[..., None] + second[2] * right_factor[..., None]
    return (highest, totals, summed)


def beacon_partial(
    queries, query_span, beacon_keys, beacon_values, low_rank, high_rank, group, slots_dev
):
    heads_local, query_count, head_size = queries.shape
    block_width = group * slots_dev
    start_state = (
        jnp.full((heads_local, query_count), LOWEST, jnp.float32),
        jnp.zeros((heads_local, query_count), jnp.float32),
        jnp.zeros((heads_local, query_count, head_size), jnp.float32),
    )

    def visit(block, state):
        first_slot = block * block_width
        block_keys = lax.dynamic_slice_in_dim(beacon_keys, first_slot, block_width, 1)
        block_values = lax.dynamic_slice_in_dim(beacon_values, first_slot, block_width, 1)
        slot_index = first_slot + jnp.arange(block_width, dtype=jnp.int32)
        owner = slot_index // slots_dev
        in_range = (owner >= low_rank) & (owner < high_rank)
        earlier = (slot_index // BEACONS)[None, :] < query_span[:, None]
        allowed = (in_range[None, :] & earlier)[None]
        return combine_partials(state, partial_attend(queries, block_keys, block_values, allowed))

    first_block = low_rank // group
    last_block = (high_rank + group - 1) // group
    return lax.fori_loop(first_block, last_block, visit, start_state)


def on_device_general(tokens_in, tempo_ids, tempo_table, w_query, w_key, w_value):
    row_count = tokens_in.shape[0]
    col_width = w_query.shape[1]
    heads_local = col_width // HEAD_DIM
    ctx_count = lax.axis_size("ctx")
    ctx_rank = lax.axis_index("ctx")
    spans_dev = row_count // SPAN
    slots_dev = spans_dev * BEACONS
    target = max(1, 256 // slots_dev)
    group = min(ctx_count, 1 << target.bit_length() - 1)
    selector = (
        tempo_ids[:, None] == jnp.arange(tempo_table.shape[0], dtype=jnp.int32)[None, :]
    ).astype(jnp.bfloat16)
    hidden = (
        tokens_in.astype(jnp.float32)
        + jnp.dot(selector, tempo_table, preferred_element_type=jnp.float32)
    ).astype(jnp.bfloat16)
    pieces = (
        lax.all_gather(w_query, "ctx", axis=0, tiled=True),
        lax.all_gather(w_key, "ctx", axis=0, tiled=True),
        lax.all_gather(w_value, "ctx", axis=0, tiled=True),
    )
    projected = tuple(
        (jnp.dot(hidden, piece, preferred_element_type=jnp.float32) for piece in pieces)
    )
    queries = projected[0].astype(jnp.bfloat16)
    keys = projected[1].astype(jnp.bfloat16)
    values = projected[2].astype(jnp.bfloat16)
    pool_scale = POOL ** (-0.5)
    own_keys = (
        jnp.sum(keys.reshape(slots_dev, POOL, col_width).astype(jnp.float32), axis=1) * pool_scale
    ).astype(jnp.bfloat16)
    own_values = (
        jnp.sum(values.reshape(slots_dev, POOL, col_width).astype(jnp.float32), axis=1) * pool_scale
    ).astype(jnp.bfloat16)
    every_keys, every_values = (
        lax.all_gather(own_keys, "ctx", axis=0, tiled=True),
        lax.all_gather(own_values, "ctx", axis=0, tiled=True),
    )
    beacon_keys = by_heads(every_keys, heads_local)
    beacon_values = by_heads(every_values, heads_local)
    query_heads = by_heads(queries, heads_local)
    local_span = jnp.arange(row_count, dtype=jnp.int32) // SPAN
    own_span = ctx_rank * spans_dev + local_span

    def fold_spans(matrix):
        return by_heads(matrix, heads_local)

    causal = (
        jnp.arange(SPAN, dtype=jnp.int32)[:, None] >= jnp.arange(SPAN, dtype=jnp.int32)[None, :]
    )[None]
    inside = partial_attend(fold_spans(queries), fold_spans(keys), fold_spans(values), causal)
    inside = (inside[0], inside[1], inside[2])
    upper_rank = ctx_rank + 1
    remote = beacon_partial(
        query_heads,
        own_span,
        beacon_keys,
        beacon_values,
        jnp.zeros((), jnp.int32),
        upper_rank,
        group,
        slots_dev,
    )
    _, totals, summed = combine_partials(inside, remote)
    attended = summed / totals[..., None]
    return attended.transpose(1, 0, 2).reshape(row_count, col_width).astype(jnp.bfloat16)


VMEM = pl.BlockSpec(memory_space=pltpu.VMEM)
HBM = pl.BlockSpec(memory_space=pltpu.HBM)


def spots():
    rank = lax.axis_index("ctx")
    return (rank, rank ^ 1, rank ^ 2, rank ^ 3, lax.axis_index("groups"))


def in_hbm(array):
    return pltpu.with_memory_space_constraint(array, pltpu.HBM)


def mm(a, b):
    return jnp.dot(a, b, preferred_element_type=jnp.float32)


def cost(flops, moved, exps=0):
    return pl.CostEstimate(flops=flops, bytes_accessed=moved, transcendentals=exps)


def limit(mebibytes):
    return pltpu.CompilerParams(vmem_limit_bytes=mebibytes << 20)


def span_of(index, size):
    return pl.ds(pl.multiple_of(index * size, size), size)


def run_copies(copies):
    for copy in copies:
        copy.start()
    for copy in copies:
        copy.wait()


def cut_kernel(*refs):
    s_ref = spots()
    count = len(refs) // 2
    sems = refs[-1]
    piece, half = refs[count].shape
    step = piece // 2
    cols = span_of(lax.rem(s_ref[0], 2), half)
    copies = []
    for source, target in zip(refs[:count], refs[count:-1]):
        for low in range(0, piece, step):
            rows = pl.ds(pl.multiple_of(s_ref[4] * piece + low, step), step)
            copies.append(
                pltpu.make_async_copy(
                    source.at[rows, cols], target.at[pl.ds(low, step)], sems.at[len(copies)]
                )
            )
    run_copies(copies)


def cut_same(*weights):
    depth, width = weights[0].shape
    count = len(weights)
    shape = jax.ShapeDtypeStruct((depth // 2, width // 2), jnp.bfloat16)
    return pl.pallas_call(
        cut_kernel,
        in_specs=[HBM] * count,
        out_specs=[VMEM] * count,
        out_shape=[shape] * count,
        scratch_shapes=[pltpu.SemaphoreType.DMA((2 * count,))],
        compiler_params=limit(1),
        cost_estimate=cost(0, count * depth * width),
        name="cut_same",
    )(*[in_hbm(w) for w in weights])


def prepare_kernel(
    ids_hbm,
    tokens_ref,
    table_hbm,
    wk_ref,
    wv_ref,
    wq_ref,
    hidden_ref,
    own_ref,
    k_here_ref,
    v_here_ref,
    there_ref,
    q_ref,
    ids_ref,
    table_ref,
    sems,
    small_sems,
    cut_sems,
):
    s_ref = spots()
    buckets, width = table_ref.shape
    rows = tokens_ref.shape[0]
    piece, half = k_here_ref.shape
    tile = TILE // 2
    step = min(width, 512)
    ahead = 3
    core = lax.rem(s_ref[0], 2)
    mine, other = span_of(core, half), span_of(1 - core, half)
    here, there = span_of(s_ref[4], piece), span_of(1 - s_ref[4], piece)
    pairs = (
        (wk_ref.at[here, other], k_here_ref),
        (wv_ref.at[here, other], v_here_ref),
        (wk_ref.at[there, other], there_ref.at[0]),
        (wv_ref.at[there, other], there_ref.at[1]),
        (wq_ref.at[:, other], q_ref),
        (wk_ref.at[:, mine], own_ref.at[0]),
        (wv_ref.at[:, mine], own_ref.at[1]),
        (wq_ref.at[:, mine], own_ref.at[2]),
    )
    cuts = [
        pltpu.make_async_copy(source, target, cut_sems.at[i])
        for i, (source, target) in enumerate(pairs)
    ]
    copies = [
        pltpu.make_async_copy(
            tokens_ref.at[pl.ds(i * tile, tile)], hidden_ref.at[pl.ds(i * tile, tile)], sems.at[i]
        )
        for i in range(rows // tile)
    ]
    small = [
        pltpu.make_async_copy(ids_hbm, ids_ref, small_sems.at[0]),
        pltpu.make_async_copy(table_hbm, table_ref, small_sems.at[1]),
    ]
    for copy in small + copies[:ahead]:
        copy.start()
    for copy in small:
        copy.wait()
    for i, copy in enumerate(copies):
        part = slice(i * tile, (i + 1) * tile)
        bucket = lax.broadcasted_iota(jnp.int32, (buckets, tile), 0)
        picked = jnp.where(bucket == ids_ref[:, part], 1.0, 0.0).astype(jnp.bfloat16)
        copy.wait()
        if i + ahead < len(copies):
            copies[i + ahead].start()
        for cut in cuts[2 * i : 2 * i + 2]:
            cut.start()
        for col in range(0, width, step):
            cols = slice(col, col + step)
            tempo = lax.dot_general(
                picked,
                table_ref[:, cols],
                (((0,), (0,)), ((), ())),
                preferred_element_type=jnp.float32,
            )
            tokens = hidden_ref[part, cols].astype(jnp.float32)
            hidden_ref[part, cols] = (tokens + tempo).astype(hidden_ref.dtype)
    for cut in cuts:
        cut.wait()


def prepare(tokens_in, tempo_ids, tempo_table, weights):
    rows, width = tokens_in.shape
    depth, full = weights[0].shape
    piece, half = depth // 2, full // 2
    shapes = (
        (rows, width),
        (3, depth, half),
        (piece, half),
        (piece, half),
        (2, piece, half),
        (depth, half),
    )
    return pl.pallas_call(
        prepare_kernel,
        in_specs=[HBM] * 6,
        out_specs=[VMEM] * 6,
        out_shape=[jax.ShapeDtypeStruct(shape, jnp.bfloat16) for shape in shapes],
        scratch_shapes=[
            pltpu.VMEM((1, rows), jnp.int32),
            pltpu.VMEM(tempo_table.shape, jnp.bfloat16),
            pltpu.SemaphoreType.DMA((2 * rows // TILE,)),
            pltpu.SemaphoreType.DMA((2,)),
            pltpu.SemaphoreType.DMA((8,)),
        ],
        compiler_params=limit(4),
        cost_estimate=cost(2 * rows * 256 * width, 4 * rows * width),
        name="prepare",
    )(
        in_hbm(tempo_ids.reshape(1, rows)),
        in_hbm(tokens_in),
        in_hbm(tempo_table),
        *[in_hbm(w) for w in weights],
    )


def local_kernel(
    hidden_ref,
    own_ref,
    k_here_ref,
    v_here_ref,
    there_ref,
    q_ref,
    kv_sum_ref,
    q_sum_ref,
    *q_halves,
):
    s_ref = spots()
    rows = hidden_ref.shape[0]
    piece, half = k_here_ref.shape
    own, mate, song = s_ref[0], s_ref[1], s_ref[4]
    for place, out_ref in enumerate(q_halves):
        out_ref[...] = q_ref[place * piece : (place + 1) * piece, :]
    for low in range(0, rows, TILE):
        part = slice(low, low + TILE)
        mine = hidden_ref[part, span_of(own, 2 * piece)]
        here = hidden_ref[part, span_of(2 * mate + song, piece)]
        there = hidden_ref[part, span_of(2 * mate + 1 - song, piece)]
        for place, here_ref in enumerate((k_here_ref, v_here_ref)):
            kv_sum_ref[part, place * half : (place + 1) * half] = (
                mm(mine, own_ref[place]) + mm(here, here_ref[...]) + mm(there, there_ref[place])
            )
        other = hidden_ref[part, span_of(mate, 2 * piece)]
        q_sum_ref[part, :] = mm(mine, own_ref[2]) + mm(other, q_ref[...])


def local_part(hidden, own_weights, mate_weights, halves):
    rows = hidden.shape[0]
    _, depth, half = own_weights.shape
    return pl.pallas_call(
        local_kernel,
        in_specs=[VMEM] * 6,
        out_specs=[VMEM] * (2 + halves),
        out_shape=[
            jax.ShapeDtypeStruct((rows, 2 * half), jnp.float32),
            jax.ShapeDtypeStruct((rows, half), jnp.float32),
        ]
        + [jax.ShapeDtypeStruct((depth // 2, half), jnp.bfloat16)] * halves,
        compiler_params=limit(6),
        cost_estimate=cost(12 * rows * depth * half, 4 * rows * depth + 12 * rows * half),
        name="local_part",
    )(hidden, own_weights, *mate_weights)


def pool_rows(rounded):
    rows, half = rounded.shape
    groups = rounded.astype(jnp.float32).reshape(rows // POOL, POOL, half)
    return (jnp.sum(groups, axis=1) * POOL ** (-0.5)).astype(jnp.bfloat16)


def early_kernel(
    own_ref,
    mate_ref,
    own_sum,
    mate_sum,
    k_mine,
    v_mine,
    k_twin,
    v_twin,
    k_far,
    v_far,
    out_ref,
):
    s_ref = spots()
    rows = own_ref.shape[0]
    piece, half = k_mine.shape
    same, cross, song = s_ref[2], s_ref[3], s_ref[4]
    weights = ((k_mine, k_twin, k_far), (v_mine, v_twin, v_far))
    for turn, (h_ref, sum_ref) in enumerate(((own_ref, own_sum), (mate_ref, mate_sum))):
        for low in range(0, rows, TILE):
            part = slice(low, low + TILE)
            target = slice(turn * rows + low, turn * rows + low + TILE)
            mine = h_ref[part, span_of(2 * same + song, piece)]
            twin = h_ref[part, span_of(2 * same + 1 - song, piece)]
            far = h_ref[part, span_of(2 * cross + song, piece)]
            for place, (w_mine, w_twin, w_far) in enumerate(weights):
                cols = slice(place * half, (place + 1) * half)
                out_ref[target, cols] = (
                    sum_ref[part, cols]
                    + mm(mine, w_mine[...])
                    + mm(twin, w_twin[...])
                    + mm(far, w_far[...])
                )


def early_sums(own, mate, sums, pieces):
    rows = own.shape[0]
    piece, half = pieces[0].shape
    return pl.pallas_call(
        early_kernel,
        in_specs=[VMEM] * 10,
        out_specs=VMEM,
        out_shape=jax.ShapeDtypeStruct((2 * rows, 2 * half), jnp.float32),
        compiler_params=limit(6),
        cost_estimate=cost(24 * rows * piece * half, 12 * rows * piece + 32 * rows * half),
        name="early_sums",
    )(own, mate, *sums, *pieces)


def late_kernel(
    own_ref, mate_ref, sum_ref, k_twin, v_twin, keys_ref, values_ref, near_ref
):
    s_ref = spots()
    rows = own_ref.shape[0]
    piece, half = k_twin.shape
    column = 2 * s_ref[3] + 1 - s_ref[4]
    for turn, h_ref in enumerate((own_ref, mate_ref)):
        for low in range(0, rows, TILE):
            hidden = h_ref[low : low + TILE, span_of(column, piece)]
            start = turn * rows + low
            target = slice(start, start + TILE)
            slots = slice(start // POOL, (start + TILE) // POOL)
            for place, (w_ref, out_ref) in enumerate(((k_twin, keys_ref), (v_twin, values_ref))):
                cols = slice(place * half, (place + 1) * half)
                rounded = (sum_ref[target, cols] + mm(hidden, w_ref[...])).astype(jnp.bfloat16)
                out_ref[target, :] = rounded
                near_ref[place, slots, :] = pool_rows(rounded)


def late_keys_values(own, mate, sums, k_twin, v_twin):
    rows = own.shape[0]
    piece, half = k_twin.shape
    return pl.pallas_call(
        late_kernel,
        in_specs=[VMEM] * 5,
        out_specs=[VMEM] * 3,
        out_shape=[
            jax.ShapeDtypeStruct((2 * rows, half), jnp.bfloat16),
            jax.ShapeDtypeStruct((2 * rows, half), jnp.bfloat16),
            jax.ShapeDtypeStruct((2, 2 * rows // POOL, half), jnp.bfloat16),
        ],
        compiler_params=limit(6),
        cost_estimate=cost(8 * rows * piece * half, 4 * rows * piece + 24 * rows * half),
        name="late_keys_values",
    )(own, mate, sums, k_twin, v_twin)


def query_kernel(columns, own_ref, mate_ref, *refs):
    s_ref = spots()
    rows = own_ref.shape[0]
    sums, weights, out_ref = refs[: -1 - len(columns)], refs[-1 - len(columns) : -1], refs[-1]
    piece = weights[0].shape[0]
    for turn, h_ref in enumerate((own_ref, mate_ref)):
        for low in range(0, rows, TILE):
            target = slice(turn * rows + low, turn * rows + low + TILE)
            if len(sums) == 2:
                total = sums[turn][low : low + TILE, :]
            else:
                total = sums[0][target, :]
            for column, w_ref in zip(columns, weights):
                total += mm(h_ref[low : low + TILE, span_of(column(s_ref), piece)], w_ref[...])
            out_ref[target, :] = total.astype(out_ref.dtype)


def query_sums(own, mate, sums, columns, pieces, dtype):
    rows = own.shape[0]
    piece, half = pieces[0].shape
    count = len(pieces)
    return pl.pallas_call(
        functools.partial(query_kernel, columns),
        in_specs=[VMEM] * (2 + len(sums) + count),
        out_specs=VMEM,
        out_shape=jax.ShapeDtypeStruct((2 * rows, half), dtype),
        compiler_params=limit(6),
        cost_estimate=cost(
            4 * count * rows * piece * half, 4 * count * rows * piece + 16 * rows * half
        ),
    )(own, mate, *sums, *pieces)


def attend_rows(
    turn, bounds, s_ref, queries_ref, keys_ref, values_ref, near_ref, far_ref, store
):
    base = turn * SPAN
    span = s_ref[turn]
    factor = HEAD_DIM ** (-0.5) * LOG2_E
    contract = (((1,), (1,)), ((), ()))
    slots = near_ref.shape[1] + far_ref.shape[1]
    owner = lax.broadcasted_iota(jnp.int32, (1, slots), 1) // BEACONS
    allowed = jnp.zeros((1, slots), jnp.int32)
    for place in range(slots // BEACONS):
        visible = (s_ref[place] < span).astype(jnp.int32)
        allowed = jnp.where(owner == place, visible, allowed)
    allowed = allowed > 0
    causal = lax.broadcasted_iota(jnp.int32, (TILE, TILE), 0) >= lax.broadcasted_iota(
        jnp.int32, (TILE, TILE), 1
    )
    start, stop = bounds
    tiles = range(start, stop, TILE)
    blocks = range(0, stop, TILE)
    heads = range(queries_ref.shape[1] // HEAD_DIM)

    def dots(query, keys):
        return lax.dot_general(query, keys, contract, preferred_element_type=jnp.float32)

    def scores(head):
        cols = slice(head * HEAD_DIM, (head + 1) * HEAD_DIM)
        query = queries_ref[base + start : base + stop, cols]
        beacon_keys = jnp.concatenate([near_ref[0, :, cols], far_ref[0, :, cols]], axis=0)
        inside = [
            dots(query[max(first - start, 0) :], keys_ref[base + first : base + first + TILE, cols])
            for first in blocks
        ]
        return dots(query, beacon_keys), inside

    def finish(head, beacon_score, inside):
        cols = slice(head * HEAD_DIM, (head + 1) * HEAD_DIM)
        amounts, beacon_weights, weights = [], [], [[] for _ in blocks]
        for low in tiles:
            row = low - start
            parts = [jnp.where(allowed, beacon_score[row : row + TILE], LOWEST)]
            for first in range(0, low + TILE, TILE):
                row = low - max(first, start)
                part = inside[first // TILE][row : row + TILE]
                parts.append(jnp.where(causal, part, LOWEST) if first == low else part)
            score = jnp.concatenate(parts, axis=1)
            highest = jnp.max(score, axis=1, keepdims=True)
            weight = jnp.exp2((score - highest) * factor)
            amounts.append(jnp.sum(weight, axis=1, keepdims=True))
            rounded = weight.astype(jnp.bfloat16)
            beacon_weights.append(rounded[:, :slots])
            for first in range(0, low + TILE, TILE):
                weights[first // TILE].append(rounded[:, slots + first : slots + first + TILE])
        beacon_values = jnp.concatenate([near_ref[1, :, cols], far_ref[1, :, cols]], axis=0)
        summed = mm(jnp.concatenate(beacon_weights, axis=0), beacon_values)
        summed = [summed[i * TILE : (i + 1) * TILE] for i in range(len(tiles))]
        for first, group in zip(blocks, weights):
            term = mm(
                jnp.concatenate(group, axis=0), values_ref[base + first : base + first + TILE, cols]
            )
            skip = len(tiles) - len(group)
            for i in range(len(group)):
                summed[skip + i] += term[i * TILE : (i + 1) * TILE]
        for low, value, amount in zip(tiles, summed, amounts):
            store(low - start, cols, value / amount)

    pending = None
    for head in heads:
        score = scores(head)
        if pending is not None:
            finish(*pending)
        pending = (head, *score)
    finish(*pending)


def attend_first_kernel(turn, bounds, *refs):
    s_ref = spots()
    out_ref = refs[-1]

    def store(row, cols, value):
        out_ref[row : row + TILE, cols] = value.astype(out_ref.dtype)

    attend_rows(turn, bounds, s_ref, *refs[:-1], store)


def attend_last_kernel(bounds, part_ref, from_mate_ref, *refs):
    s_ref = spots()
    out_ref, scratch, sems = refs[-3:]
    start, stop = bounds
    half = scratch.shape[1]
    core = lax.rem(s_ref[0], 2)
    mine, other = span_of(core, half), span_of(1 - core, half)
    middle = stop // 2
    copies = [
        pltpu.make_async_copy(part_ref, out_ref.at[pl.ds(0, start), mine], sems.at[0]),
    ] + [
        pltpu.make_async_copy(
            from_mate_ref.at[pl.ds(low, middle)],
            out_ref.at[pl.ds(low, middle), other],
            sems.at[1 + low // middle],
        )
        for low in (0, middle)
    ]
    for copy in copies:
        copy.start()

    def store(row, cols, value):
        scratch[row : row + TILE, cols] = value.astype(scratch.dtype)
        if cols.stop == half:
            copy = pltpu.make_async_copy(
                scratch.at[pl.ds(row, TILE)],
                out_ref.at[pl.ds(start + row, TILE), mine],
                sems.at[3 + row // TILE],
            )
            copy.start()
            copies.append(copy)

    attend_rows(0, bounds, s_ref, *refs[:-3], store)
    for copy in copies:
        copy.wait()


def attend(kernel, bounds, arrays, out_spec, shape, scratch=()):
    width = shape[1]
    area = (bounds[1] - bounds[0]) * bounds[1]
    return pl.pallas_call(
        kernel,
        in_specs=[VMEM] * len(arrays),
        out_specs=out_spec,
        out_shape=jax.ShapeDtypeStruct(shape, jnp.bfloat16),
        scratch_shapes=list(scratch),
        compiler_params=limit(12),
        cost_estimate=cost(4 * area * width, 8 * shape[0] * width, area * width // HEAD_DIM),
    )(*arrays)


def on_device(tokens_in, tempo_ids, tempo_table, w_query, w_key, w_value):
    _, width = w_key.shape
    rows = tokens_in.shape[0]
    half = width // 2
    ranks = range(lax.axis_size("ctx"))
    weights = (w_key, w_value, w_query)

    def to_mate(array):
        return lax.ppermute(array, "ctx", [(r, r ^ 1) for r in ranks])

    def to_far(array):
        return lax.ppermute(array, "ctx", [(r, r ^ 2) for r in ranks])

    def to_twin(array):
        return lax.ppermute(array, "groups", [(0, 1), (1, 0)])

    k_cut, v_cut, q_cut = cut_same(*weights)
    own, own_weights, *cuts = prepare(tokens_in, tempo_ids, tempo_table, weights)
    k_mine = to_far(k_cut)
    v_mine = to_far(v_cut)
    q_mine = to_far(q_cut)
    mate_k = to_mate(cuts[0])
    mate_v = to_mate(cuts[1])
    mate_there = to_mate(cuts[2])
    mate_q = to_mate(cuts[3])
    mate = to_mate(own)
    k_far_mine = to_far(mate_k)
    v_far_mine = to_far(mate_v)
    k_twin = to_twin(k_mine)
    v_twin = to_twin(v_mine)
    k_far_twin = to_twin(k_far_mine)
    v_far_twin = to_twin(v_far_mine)
    q_same_twin = to_twin(q_mine)

    mate_weights = (mate_k, mate_v, mate_there, mate_q)
    own_kv, own_q, *q_halves = local_part(own, own_weights, mate_weights, 2)
    q_cross0 = to_far(q_halves[0])
    q_cross1 = to_far(q_halves[1])
    mate_kv, mate_q_sum = local_part(mate, own_weights, mate_weights, 0)
    pieces = (k_mine, v_mine, k_twin, v_twin, k_far_mine, v_far_mine)
    kv_sums = early_sums(own, mate, (own_kv, mate_kv), pieces)
    keys, values, near = late_keys_values(
        own, mate, kv_sums, k_far_twin, v_far_twin
    )
    far = to_far(near)

    def add_queries(sums, parts, dtype):
        columns, pieces = zip(*parts)
        return query_sums(own, mate, sums, columns, pieces, dtype)

    same_mine = (lambda s: 2 * s[2] + s[4], q_mine)
    same_twin = (lambda s: 2 * s[2] + 1 - s[4], q_same_twin)
    cross = [(lambda s: 2 * s[3], q_cross0), (lambda s: 2 * s[3] + 1, q_cross1)]
    q_sums = add_queries((own_q, mate_q_sum), (same_mine, cross[0]), jnp.float32)
    q_sums = add_queries((q_sums,), (same_twin,), jnp.float32)
    queries = add_queries((q_sums,), (cross[1],), jnp.bfloat16)
    rest = (queries, keys, values, near, far)
    middle = rows - TILE
    kernel = functools.partial(attend_first_kernel, 1, (0, rows))
    arrays = rest
    for_mate = attend(kernel, (0, rows), arrays, VMEM, (rows, half))
    from_mate = to_mate(for_mate)
    kernel = functools.partial(attend_first_kernel, 0, (0, middle))
    arrays = rest
    part = attend(kernel, (0, middle), arrays, VMEM, (middle, half))
    scratch = (
        pltpu.VMEM((rows - middle, half), jnp.bfloat16),
        pltpu.SemaphoreType.DMA((3 + (rows - middle) // TILE,)),
    )
    bounds = (middle, rows)
    kernel = functools.partial(attend_last_kernel, bounds)
    arrays = (part, from_mate, *rest)
    return attend(kernel, bounds, arrays, HBM, (rows, width), scratch)


def fits(mesh):
    return mesh.shape["ctx"] == 4 and mesh.shape["groups"] == 2


def solution(mesh):
    in_specs = (
        P(("groups", "ctx"), None),
        P(("groups", "ctx")),
        P(),
        P("ctx", "head"),
        P("ctx", "head"),
        P("ctx", "head"),
    )
    out_specs = P(("groups", "ctx"), "head")

    planned = fits(mesh)

    def body(*arrays):
        return (on_device if planned else on_device_general)(*arrays)

    return jax.shard_map(
        body, mesh=mesh, in_specs=in_specs, out_specs=out_specs, check_vma=False
    )
```

```python
import functools

import jax
import jax.numpy as jnp
from jax import lax
from jax.experimental import pallas as pl
from jax.experimental.pallas import tpu as pltpu
from jax.sharding import PartitionSpec as P

HEAD_DIM = 128
SPAN = 1024
BEACONS = 32
POOL = 32


LOWEST = -1e30
LOG2_E = 1.4426950408889634
TILE = 256


def by_heads(matrix, heads_local):
    return matrix.reshape(matrix.shape[0], heads_local, -1).transpose(1, 0, 2)


def partial_attend(queries, keys, values, allowed):
    scores = jnp.einsum(
        "hqd,hkd->hqk", queries, keys, preferred_element_type=jnp.float32
    ) * queries.shape[-1] ** (-0.5)
    masked = jnp.where(allowed, scores, LOWEST)
    highest = jnp.max(masked, axis=2)
    weights = jnp.where(allowed, jnp.exp(masked - highest[..., None]), 0.0)
    totals = jnp.sum(weights, axis=2)
    summed = jnp.einsum(
        "hqk,hkd->hqd", weights.astype(jnp.bfloat16), values, preferred_element_type=jnp.float32
    )
    return (highest, totals, summed)


def combine_partials(first, second):
    highest = jnp.maximum(first[0], second[0])
    left_factor = jnp.exp(first[0] - highest)
    right_factor = jnp.exp(second[0] - highest)
    totals = first[1] * left_factor + second[1] * right_factor
    summed = first[2] * left_factor[..., None] + second[2] * right_factor[..., None]
    return (highest, totals, summed)


def beacon_partial(
    queries, query_span, beacon_keys, beacon_values, low_rank, high_rank, group, slots_dev
):
    heads_local, query_count, head_size = queries.shape
    block_width = group * slots_dev
    start_state = (
        jnp.full((heads_local, query_count), LOWEST, jnp.float32),
        jnp.zeros((heads_local, query_count), jnp.float32),
        jnp.zeros((heads_local, query_count, head_size), jnp.float32),
    )

    def visit(block, state):
        first_slot = block * block_width
        block_keys = lax.dynamic_slice_in_dim(beacon_keys, first_slot, block_width, 1)
        block_values = lax.dynamic_slice_in_dim(beacon_values, first_slot, block_width, 1)
        slot_index = first_slot + jnp.arange(block_width, dtype=jnp.int32)
        owner = slot_index // slots_dev
        in_range = (owner >= low_rank) & (owner < high_rank)
        earlier = (slot_index // BEACONS)[None, :] < query_span[:, None]
        allowed = (in_range[None, :] & earlier)[None]
        return combine_partials(state, partial_attend(queries, block_keys, block_values, allowed))

    first_block = low_rank // group
    last_block = (high_rank + group - 1) // group
    return lax.fori_loop(first_block, last_block, visit, start_state)


def on_device_general(tokens_in, tempo_ids, tempo_table, w_query, w_key, w_value):
    row_count = tokens_in.shape[0]
    col_width = w_query.shape[1]
    heads_local = col_width // HEAD_DIM
    ctx_count = lax.axis_size("ctx")
    ctx_rank = lax.axis_index("ctx")
    spans_dev = row_count // SPAN
    slots_dev = spans_dev * BEACONS
    target = max(1, 256 // slots_dev)
    group = min(ctx_count, 1 << target.bit_length() - 1)
    selector = (
        tempo_ids[:, None] == jnp.arange(tempo_table.shape[0], dtype=jnp.int32)[None, :]
    ).astype(jnp.bfloat16)
    hidden = (
        tokens_in.astype(jnp.float32)
        + jnp.dot(selector, tempo_table, preferred_element_type=jnp.float32)
    ).astype(jnp.bfloat16)
    pieces = (
        lax.all_gather(w_query, "ctx", axis=0, tiled=True),
        lax.all_gather(w_key, "ctx", axis=0, tiled=True),
        lax.all_gather(w_value, "ctx", axis=0, tiled=True),
    )
    projected = tuple(
        (jnp.dot(hidden, piece, preferred_element_type=jnp.float32) for piece in pieces)
    )
    queries = projected[0].astype(jnp.bfloat16)
    keys = projected[1].astype(jnp.bfloat16)
    values = projected[2].astype(jnp.bfloat16)
    pool_scale = POOL ** (-0.5)
    own_keys = (
        jnp.sum(keys.reshape(slots_dev, POOL, col_width).astype(jnp.float32), axis=1) * pool_scale
    ).astype(jnp.bfloat16)
    own_values = (
        jnp.sum(values.reshape(slots_dev, POOL, col_width).astype(jnp.float32), axis=1) * pool_scale
    ).astype(jnp.bfloat16)
    every_keys, every_values = (
        lax.all_gather(own_keys, "ctx", axis=0, tiled=True),
        lax.all_gather(own_values, "ctx", axis=0, tiled=True),
    )
    beacon_keys = by_heads(every_keys, heads_local)
    beacon_values = by_heads(every_values, heads_local)
    query_heads = by_heads(queries, heads_local)
    local_span = jnp.arange(row_count, dtype=jnp.int32) // SPAN
    own_span = ctx_rank * spans_dev + local_span

    def fold_spans(matrix):
        return by_heads(matrix, heads_local)

    causal = (
        jnp.arange(SPAN, dtype=jnp.int32)[:, None] >= jnp.arange(SPAN, dtype=jnp.int32)[None, :]
    )[None]
    inside = partial_attend(fold_spans(queries), fold_spans(keys), fold_spans(values), causal)
    inside = (inside[0], inside[1], inside[2])
    upper_rank = ctx_rank + 1
    remote = beacon_partial(
        query_heads,
        own_span,
        beacon_keys,
        beacon_values,
        jnp.zeros((), jnp.int32),
        upper_rank,
        group,
        slots_dev,
    )
    _, totals, summed = combine_partials(inside, remote)
    attended = summed / totals[..., None]
    return attended.transpose(1, 0, 2).reshape(row_count, col_width).astype(jnp.bfloat16)


VMEM = pl.BlockSpec(memory_space=pltpu.VMEM)
HBM = pl.BlockSpec(memory_space=pltpu.HBM)


def spots():
    rank = lax.axis_index("ctx")
    return (rank, rank ^ 1, rank ^ 2, rank ^ 3, lax.axis_index("groups"))


def in_hbm(array):
    return pltpu.with_memory_space_constraint(array, pltpu.HBM)


def mm(a, b):
    return jnp.dot(a, b, preferred_element_type=jnp.float32)


def cost(flops, moved, exps=0):
    return pl.CostEstimate(flops=flops, bytes_accessed=moved, transcendentals=exps)


def limit(mebibytes):
    return pltpu.CompilerParams(vmem_limit_bytes=mebibytes << 20)


def span_of(index, size):
    return pl.ds(pl.multiple_of(index * size, size), size)


def run_copies(copies):
    for copy in copies:
        copy.start()
    for copy in copies:
        copy.wait()


def cut_kernel(*refs):
    s_ref = spots()
    count = len(refs) // 2
    sems = refs[-1]
    piece, half = refs[count].shape
    step = piece // 2
    cols = span_of(lax.rem(s_ref[0], 2), half)
    copies = []
    for source, target in zip(refs[:count], refs[count:-1]):
        for low in range(0, piece, step):
            rows = pl.ds(pl.multiple_of(s_ref[4] * piece + low, step), step)
            copies.append(
                pltpu.make_async_copy(
                    source.at[rows, cols], target.at[pl.ds(low, step)], sems.at[len(copies)]
                )
            )
    run_copies(copies)


def cut_same(*weights):
    depth, width = weights[0].shape
    count = len(weights)
    shape = jax.ShapeDtypeStruct((depth // 2, width // 2), jnp.bfloat16)
    return pl.pallas_call(
        cut_kernel,
        in_specs=[HBM] * count,
        out_specs=[VMEM] * count,
        out_shape=[shape] * count,
        scratch_shapes=[pltpu.SemaphoreType.DMA((2 * count,))],
        compiler_params=limit(1),
        cost_estimate=cost(0, count * depth * width),
        name="cut_same",
    )(*[in_hbm(w) for w in weights])


def prepare_kernel(
    ids_hbm,
    tokens_ref,
    table_hbm,
    wk_ref,
    wv_ref,
    wq_ref,
    hidden_ref,
    own_ref,
    k_here_ref,
    v_here_ref,
    there_ref,
    q_ref,
    ids_ref,
    table_ref,
    sems,
    small_sems,
    cut_sems,
):
    s_ref = spots()
    buckets, width = table_ref.shape
    rows = tokens_ref.shape[0]
    piece, half = k_here_ref.shape
    tile = TILE // 2
    step = min(width, 512)
    ahead = 3
    core = lax.rem(s_ref[0], 2)
    mine, other = span_of(core, half), span_of(1 - core, half)
    here, there = span_of(s_ref[4], piece), span_of(1 - s_ref[4], piece)
    pairs = (
        (wk_ref.at[here, other], k_here_ref),
        (wv_ref.at[here, other], v_here_ref),
        (wk_ref.at[there, other], there_ref.at[0]),
        (wv_ref.at[there, other], there_ref.at[1]),
        (wq_ref.at[:, other], q_ref),
        (wk_ref.at[:, mine], own_ref.at[0]),
        (wv_ref.at[:, mine], own_ref.at[1]),
        (wq_ref.at[:, mine], own_ref.at[2]),
    )
    cuts = [
        pltpu.make_async_copy(source, target, cut_sems.at[i])
        for i, (source, target) in enumerate(pairs)
    ]
    copies = [
        pltpu.make_async_copy(
            tokens_ref.at[pl.ds(i * tile, tile)], hidden_ref.at[pl.ds(i * tile, tile)], sems.at[i]
        )
        for i in range(rows // tile)
    ]
    small = [
        pltpu.make_async_copy(ids_hbm, ids_ref, small_sems.at[0]),
        pltpu.make_async_copy(table_hbm, table_ref, small_sems.at[1]),
    ]
    for copy in small + copies[:ahead]:
        copy.start()
    for copy in small:
        copy.wait()
    for i, copy in enumerate(copies):
        part = slice(i * tile, (i + 1) * tile)
        bucket = lax.broadcasted_iota(jnp.int32, (buckets, tile), 0)
        picked = jnp.where(bucket == ids_ref[:, part], 1.0, 0.0).astype(jnp.bfloat16)
        copy.wait()
        if i + ahead < len(copies):
            copies[i + ahead].start()
        for cut in cuts[2 * i : 2 * i + 2]:
            cut.start()
        for col in range(0, width, step):
            cols = slice(col, col + step)
            tempo = lax.dot_general(
                picked,
                table_ref[:, cols],
                (((0,), (0,)), ((), ())),
                preferred_element_type=jnp.float32,
            )
            tokens = hidden_ref[part, cols].astype(jnp.float32)
            hidden_ref[part, cols] = (tokens + tempo).astype(hidden_ref.dtype)
    for cut in cuts:
        cut.wait()


def prepare(tokens_in, tempo_ids, tempo_table, weights):
    rows, width = tokens_in.shape
    depth, full = weights[0].shape
    piece, half = depth // 2, full // 2
    shapes = (
        (rows, width),
        (3, depth, half),
        (piece, half),
        (piece, half),
        (2, piece, half),
        (depth, half),
    )
    return pl.pallas_call(
        prepare_kernel,
        in_specs=[HBM] * 6,
        out_specs=[VMEM] * 6,
        out_shape=[jax.ShapeDtypeStruct(shape, jnp.bfloat16) for shape in shapes],
        scratch_shapes=[
            pltpu.VMEM((1, rows), jnp.int32),
            pltpu.VMEM(tempo_table.shape, jnp.bfloat16),
            pltpu.SemaphoreType.DMA((2 * rows // TILE,)),
            pltpu.SemaphoreType.DMA((2,)),
            pltpu.SemaphoreType.DMA((8,)),
        ],
        compiler_params=limit(4),
        cost_estimate=cost(2 * rows * 256 * width, 4 * rows * width),
        name="prepare",
    )(
        in_hbm(tempo_ids.reshape(1, rows)),
        in_hbm(tokens_in),
        in_hbm(tempo_table),
        *[in_hbm(w) for w in weights],
    )


def local_kernel(
    hidden_ref,
    own_ref,
    k_here_ref,
    v_here_ref,
    there_ref,
    q_ref,
    kv_sum_ref,
    q_sum_ref,
    *q_parts,
):
    s_ref = spots()
    rows = hidden_ref.shape[0]
    piece, half = k_here_ref.shape
    own, mate, song = s_ref[0], s_ref[1], s_ref[4]
    first = 0
    for out_ref in q_parts:
        out_ref[...] = q_ref[first : first + out_ref.shape[0], :]
        first += out_ref.shape[0]
    for low in range(0, rows, TILE):
        part = slice(low, low + TILE)
        mine = hidden_ref[part, span_of(own, 2 * piece)]
        here = hidden_ref[part, span_of(2 * mate + song, piece)]
        there = hidden_ref[part, span_of(2 * mate + 1 - song, piece)]
        for place, here_ref in enumerate((k_here_ref, v_here_ref)):
            kv_sum_ref[part, place * half : (place + 1) * half] = (
                mm(mine, own_ref[place]) + mm(here, here_ref[...]) + mm(there, there_ref[place])
            )
        other = hidden_ref[part, span_of(mate, 2 * piece)]
        q_sum_ref[part, :] = mm(mine, own_ref[2]) + mm(other, q_ref[...])


def local_part(hidden, own_weights, mate_weights, parts):
    rows = hidden.shape[0]
    _, depth, half = own_weights.shape
    return pl.pallas_call(
        local_kernel,
        in_specs=[VMEM] * 6,
        out_specs=[VMEM] * (2 + len(parts)),
        out_shape=[
            jax.ShapeDtypeStruct((rows, 2 * half), jnp.float32),
            jax.ShapeDtypeStruct((rows, half), jnp.float32),
        ]
        + [jax.ShapeDtypeStruct((count, half), jnp.bfloat16) for count in parts],
        compiler_params=limit(6),
        cost_estimate=cost(12 * rows * depth * half, 4 * rows * depth + 12 * rows * half),
        name="local_part",
    )(hidden, own_weights, *mate_weights)


def pool_rows(rounded):
    rows, half = rounded.shape
    groups = rounded.astype(jnp.float32).reshape(rows // POOL, POOL, half)
    return (jnp.sum(groups, axis=1) * POOL ** (-0.5)).astype(jnp.bfloat16)


def early_kernel(
    own_ref,
    mate_ref,
    own_sum,
    mate_sum,
    k_mine,
    v_mine,
    k_twin,
    v_twin,
    k_far,
    v_far,
    out_ref,
):
    s_ref = spots()
    rows = own_ref.shape[0]
    piece, half = k_mine.shape
    same, cross, song = s_ref[2], s_ref[3], s_ref[4]
    weights = ((k_mine, k_twin, k_far), (v_mine, v_twin, v_far))
    for turn, (h_ref, sum_ref) in enumerate(((own_ref, own_sum), (mate_ref, mate_sum))):
        for low in range(0, rows, TILE):
            part = slice(low, low + TILE)
            target = slice(turn * rows + low, turn * rows + low + TILE)
            mine = h_ref[part, span_of(2 * same + song, piece)]
            twin = h_ref[part, span_of(2 * same + 1 - song, piece)]
            far = h_ref[part, span_of(2 * cross + song, piece)]
            for place, (w_mine, w_twin, w_far) in enumerate(weights):
                cols = slice(place * half, (place + 1) * half)
                out_ref[target, cols] = (
                    sum_ref[part, cols]
                    + mm(mine, w_mine[...])
                    + mm(twin, w_twin[...])
                    + mm(far, w_far[...])
                )


def early_sums(own, mate, sums, pieces):
    rows = own.shape[0]
    piece, half = pieces[0].shape
    return pl.pallas_call(
        early_kernel,
        in_specs=[VMEM] * 10,
        out_specs=VMEM,
        out_shape=jax.ShapeDtypeStruct((2 * rows, 2 * half), jnp.float32),
        compiler_params=limit(6),
        cost_estimate=cost(24 * rows * piece * half, 12 * rows * piece + 32 * rows * half),
        name="early_sums",
    )(own, mate, *sums, *pieces)


def late_kernel(
    own_ref, mate_ref, sum_ref, k_twin, v_twin, keys_ref, values_ref, near_ref
):
    s_ref = spots()
    rows = own_ref.shape[0]
    piece, half = k_twin.shape
    column = 2 * s_ref[3] + 1 - s_ref[4]
    for turn, h_ref in enumerate((own_ref, mate_ref)):
        for low in range(0, rows, TILE):
            hidden = h_ref[low : low + TILE, span_of(column, piece)]
            start = turn * rows + low
            target = slice(start, start + TILE)
            slots = slice(start // POOL, (start + TILE) // POOL)
            for place, (w_ref, out_ref) in enumerate(((k_twin, keys_ref), (v_twin, values_ref))):
                cols = slice(place * half, (place + 1) * half)
                rounded = (sum_ref[target, cols] + mm(hidden, w_ref[...])).astype(jnp.bfloat16)
                out_ref[target, :] = rounded
                near_ref[place, slots, :] = pool_rows(rounded)


def late_keys_values(own, mate, sums, k_twin, v_twin):
    rows = own.shape[0]
    piece, half = k_twin.shape
    return pl.pallas_call(
        late_kernel,
        in_specs=[VMEM] * 5,
        out_specs=[VMEM] * 3,
        out_shape=[
            jax.ShapeDtypeStruct((2 * rows, half), jnp.bfloat16),
            jax.ShapeDtypeStruct((2 * rows, half), jnp.bfloat16),
            jax.ShapeDtypeStruct((2, 2 * rows // POOL, half), jnp.bfloat16),
        ],
        compiler_params=limit(6),
        cost_estimate=cost(8 * rows * piece * half, 4 * rows * piece + 24 * rows * half),
        name="late_keys_values",
    )(own, mate, sums, k_twin, v_twin)


def query_kernel(columns, own_ref, mate_ref, *refs):
    s_ref = spots()
    rows = own_ref.shape[0]
    sums, weights, out_ref = refs[: -1 - len(columns)], refs[-1 - len(columns) : -1], refs[-1]
    for turn, h_ref in enumerate((own_ref, mate_ref)):
        for low in range(0, rows, TILE):
            target = slice(turn * rows + low, turn * rows + low + TILE)
            if len(sums) == 2:
                total = sums[turn][low : low + TILE, :]
            else:
                total = sums[0][target, :]
            for column, w_ref in zip(columns, weights):
                cols = pl.ds(pl.multiple_of(column(s_ref), TILE), w_ref.shape[0])
                total += mm(h_ref[low : low + TILE, cols], w_ref[...])
            out_ref[target, :] = total.astype(out_ref.dtype)


def query_sums(own, mate, sums, columns, pieces, dtype):
    rows = own.shape[0]
    half = pieces[0].shape[1]
    deep = sum(piece.shape[0] for piece in pieces)
    return pl.pallas_call(
        functools.partial(query_kernel, columns),
        in_specs=[VMEM] * (2 + len(sums) + len(pieces)),
        out_specs=VMEM,
        out_shape=jax.ShapeDtypeStruct((2 * rows, half), dtype),
        compiler_params=limit(6),
        cost_estimate=cost(4 * rows * deep * half, 4 * rows * deep + 16 * rows * half),
    )(own, mate, *sums, *pieces)


def attend_rows(
    turn, bounds, s_ref, queries_ref, keys_ref, values_ref, near_ref, far_ref, store
):
    base = turn * SPAN
    span = s_ref[turn]
    factor = HEAD_DIM ** (-0.5) * LOG2_E
    contract = (((1,), (1,)), ((), ()))
    slots = near_ref.shape[1] + far_ref.shape[1]
    owner = lax.broadcasted_iota(jnp.int32, (1, slots), 1) // BEACONS
    allowed = jnp.zeros((1, slots), jnp.int32)
    for place in range(slots // BEACONS):
        visible = (s_ref[place] < span).astype(jnp.int32)
        allowed = jnp.where(owner == place, visible, allowed)
    allowed = allowed > 0
    causal = lax.broadcasted_iota(jnp.int32, (TILE, TILE), 0) >= lax.broadcasted_iota(
        jnp.int32, (TILE, TILE), 1
    )
    start, stop = bounds
    tiles = range(start, stop, TILE)
    blocks = range(0, stop, TILE)
    heads = range(queries_ref.shape[1] // HEAD_DIM)

    def dots(query, keys):
        return lax.dot_general(query, keys, contract, preferred_element_type=jnp.float32)

    def scores(head):
        cols = slice(head * HEAD_DIM, (head + 1) * HEAD_DIM)
        query = queries_ref[base + start : base + stop, cols]
        beacon_keys = jnp.concatenate([near_ref[0, :, cols], far_ref[0, :, cols]], axis=0)
        beacon_score = dots(query, beacon_keys)
        inside = [
            dots(query[max(first - start, 0) :], keys_ref[base + first : base + first + TILE, cols])
            for first in blocks
        ]
        return beacon_score, inside

    def finish(head, beacon_score, inside):
        cols = slice(head * HEAD_DIM, (head + 1) * HEAD_DIM)
        amounts, beacon_weights, weights = [], [], [[] for _ in blocks]
        for low in tiles:
            row = low - start
            parts = [jnp.where(allowed, beacon_score[row : row + TILE], LOWEST)]
            for first in range(0, low + TILE, TILE):
                row = low - max(first, start)
                part = inside[first // TILE][row : row + TILE]
                parts.append(jnp.where(causal, part, LOWEST) if first == low else part)
            score = jnp.concatenate(parts, axis=1)
            highest = jnp.max(score, axis=1, keepdims=True)
            weight = jnp.exp2((score - highest) * factor)
            amounts.append(jnp.sum(weight, axis=1, keepdims=True))
            rounded = weight.astype(jnp.bfloat16)
            beacon_weights.append(rounded[:, :slots])
            for first in range(0, low + TILE, TILE):
                weights[first // TILE].append(rounded[:, slots + first : slots + first + TILE])
        beacon_values = jnp.concatenate([near_ref[1, :, cols], far_ref[1, :, cols]], axis=0)
        summed = mm(jnp.concatenate(beacon_weights, axis=0), beacon_values)
        summed = [summed[i * TILE : (i + 1) * TILE] for i in range(len(tiles))]
        for first, group in zip(blocks, weights):
            term = mm(
                jnp.concatenate(group, axis=0), values_ref[base + first : base + first + TILE, cols]
            )
            skip = len(tiles) - len(group)
            for i in range(len(group)):
                summed[skip + i] += term[i * TILE : (i + 1) * TILE]
        for low, value, amount in zip(tiles, summed, amounts):
            store(low - start, cols, value / amount)

    pending = None
    for head in heads:
        score = scores(head)
        if pending is not None:
            finish(*pending)
        pending = (head, *score)
    finish(*pending)


def attend_first_kernel(turn, bounds, *refs):
    s_ref = spots()
    out_ref = refs[-1]

    def store(row, cols, value):
        out_ref[row : row + TILE, cols] = value.astype(out_ref.dtype)

    attend_rows(turn, bounds, s_ref, *refs[:-1], store)


def attend_last_kernel(bounds, part_ref, from_mate_ref, *refs):
    s_ref = spots()
    out_ref, scratch, sems = refs[-3:]
    start, stop = bounds
    half = scratch.shape[1]
    core = lax.rem(s_ref[0], 2)
    mine, other = span_of(core, half), span_of(1 - core, half)
    middle = stop // 2
    copies = [
        pltpu.make_async_copy(part_ref, out_ref.at[pl.ds(0, start), mine], sems.at[0]),
    ] + [
        pltpu.make_async_copy(
            from_mate_ref.at[pl.ds(low, middle)],
            out_ref.at[pl.ds(low, middle), other],
            sems.at[1 + low // middle],
        )
        for low in (0, middle)
    ]
    for copy in copies:
        copy.start()

    def store(row, cols, value):
        scratch[row : row + TILE, cols] = value.astype(scratch.dtype)
        if cols.stop == half:
            copy = pltpu.make_async_copy(
                scratch.at[pl.ds(row, TILE)],
                out_ref.at[pl.ds(start + row, TILE), mine],
                sems.at[3 + row // TILE],
            )
            copy.start()
            copies.append(copy)

    attend_rows(0, bounds, s_ref, *refs[:-3], store)
    for copy in copies:
        copy.wait()


def attend(kernel, bounds, arrays, out_spec, shape, scratch=()):
    width = shape[1]
    area = (bounds[1] - bounds[0]) * bounds[1]
    return pl.pallas_call(
        kernel,
        in_specs=[VMEM] * len(arrays),
        out_specs=out_spec,
        out_shape=jax.ShapeDtypeStruct(shape, jnp.bfloat16),
        scratch_shapes=list(scratch),
        compiler_params=limit(12),
        cost_estimate=cost(4 * area * width, 8 * shape[0] * width, area * width // HEAD_DIM),
    )(*arrays)


def on_device(tokens_in, tempo_ids, tempo_table, w_query, w_key, w_value):
    depth, width = w_key.shape
    rows = tokens_in.shape[0]
    half = width // 2
    piece = depth // 2
    ranks = range(lax.axis_size("ctx"))
    weights = (w_key, w_value, w_query)

    def to_mate(array):
        return lax.ppermute(array, "ctx", [(r, r ^ 1) for r in ranks])

    def to_far(array):
        return lax.ppermute(array, "ctx", [(r, r ^ 2) for r in ranks])

    def to_twin(array):
        return lax.ppermute(array, "groups", [(0, 1), (1, 0)])

    k_cut, v_cut, q_cut = cut_same(*weights)
    own, own_weights, *cuts = prepare(tokens_in, tempo_ids, tempo_table, weights)
    k_mine = to_far(k_cut)
    v_mine = to_far(v_cut)
    q_mine = to_far(q_cut)
    mate_k = to_mate(cuts[0])
    mate_v = to_mate(cuts[1])
    mate_there = to_mate(cuts[2])
    mate_q = to_mate(cuts[3])
    mate = to_mate(own)
    k_far_mine = to_far(mate_k)
    v_far_mine = to_far(mate_v)
    k_twin = to_twin(k_mine)
    v_twin = to_twin(v_mine)
    k_far_twin = to_twin(k_far_mine)
    v_far_twin = to_twin(v_far_mine)
    q_same_twin = to_twin(q_mine)

    mate_weights = (mate_k, mate_v, mate_there, mate_q)
    parts = (depth - depth // 4, depth // 4)
    own_kv, own_q, *q_parts = local_part(own, own_weights, mate_weights, parts)
    q_cross0 = to_far(q_parts[0])
    q_cross1 = to_far(q_parts[1])
    mate_kv, mate_q_sum = local_part(mate, own_weights, mate_weights, ())
    pieces = (k_mine, v_mine, k_twin, v_twin, k_far_mine, v_far_mine)
    kv_sums = early_sums(own, mate, (own_kv, mate_kv), pieces)
    keys, values, near = late_keys_values(
        own, mate, kv_sums, k_far_twin, v_far_twin
    )
    far = to_far(near)

    def add_queries(sums, parts, dtype):
        columns, pieces = zip(*parts)
        return query_sums(own, mate, sums, columns, pieces, dtype)

    same_mine = (lambda s: (2 * s[2] + s[4]) * piece, q_mine)
    same_twin = (lambda s: (2 * s[2] + 1 - s[4]) * piece, q_same_twin)
    cross = [
        (lambda s: s[3] * depth, q_cross0),
        (lambda s: s[3] * depth + parts[0], q_cross1),
    ]
    q_sums = add_queries((own_q, mate_q_sum), (same_mine, cross[0]), jnp.float32)
    q_sums = add_queries((q_sums,), (same_twin,), jnp.float32)
    queries = add_queries((q_sums,), (cross[1],), jnp.bfloat16)
    rest = (queries, keys, values, near, far)
    middle = rows - TILE
    kernel = functools.partial(attend_first_kernel, 1, (0, rows))
    arrays = rest
    for_mate = attend(kernel, (0, rows), arrays, VMEM, (rows, half))
    from_mate = to_mate(for_mate)
    kernel = functools.partial(attend_first_kernel, 0, (0, middle))
    arrays = rest
    part = attend(kernel, (0, middle), arrays, VMEM, (middle, half))
    scratch = (
        pltpu.VMEM((rows - middle, half), jnp.bfloat16),
        pltpu.SemaphoreType.DMA((3 + (rows - middle) // TILE,)),
    )
    bounds = (middle, rows)
    kernel = functools.partial(attend_last_kernel, bounds)
    arrays = (part, from_mate, *rest)
    return attend(kernel, bounds, arrays, HBM, (rows, width), scratch)


def fits(mesh):
    return mesh.shape["ctx"] == 4 and mesh.shape["groups"] == 2


def solution(mesh):
    in_specs = (
        P(("groups", "ctx"), None),
        P(("groups", "ctx")),
        P(),
        P("ctx", "head"),
        P("ctx", "head"),
        P("ctx", "head"),
    )
    out_specs = P(("groups", "ctx"), "head")

    planned = fits(mesh)

    def body(*arrays):
        return (on_device if planned else on_device_general)(*arrays)

    return jax.shard_map(
        body, mesh=mesh, in_specs=in_specs, out_specs=out_specs, check_vma=False
    )
```

```python
import functools

import jax
import jax.numpy as jnp
from jax import lax
from jax.experimental import pallas as pl
from jax.experimental.pallas import tpu as pltpu
from jax.sharding import PartitionSpec as P

HEAD_DIM = 128
SPAN = 1024
BEACONS = 32
POOL = 32


LOWEST = -1e30
LOG2_E = 1.4426950408889634
TILE = 256


def by_heads(matrix, heads_local):
    return matrix.reshape(matrix.shape[0], heads_local, -1).transpose(1, 0, 2)


def partial_attend(queries, keys, values, allowed):
    scores = jnp.einsum(
        "hqd,hkd->hqk", queries, keys, preferred_element_type=jnp.float32
    ) * queries.shape[-1] ** (-0.5)
    masked = jnp.where(allowed, scores, LOWEST)
    highest = jnp.max(masked, axis=2)
    weights = jnp.where(allowed, jnp.exp(masked - highest[..., None]), 0.0)
    totals = jnp.sum(weights, axis=2)
    summed = jnp.einsum(
        "hqk,hkd->hqd", weights.astype(jnp.bfloat16), values, preferred_element_type=jnp.float32
    )
    return (highest, totals, summed)


def combine_partials(first, second):
    highest = jnp.maximum(first[0], second[0])
    left_factor = jnp.exp(first[0] - highest)
    right_factor = jnp.exp(second[0] - highest)
    totals = first[1] * left_factor + second[1] * right_factor
    summed = first[2] * left_factor[..., None] + second[2] * right_factor[..., None]
    return (highest, totals, summed)


def beacon_partial(
    queries, query_span, beacon_keys, beacon_values, low_rank, high_rank, group, slots_dev
):
    heads_local, query_count, head_size = queries.shape
    block_width = group * slots_dev
    start_state = (
        jnp.full((heads_local, query_count), LOWEST, jnp.float32),
        jnp.zeros((heads_local, query_count), jnp.float32),
        jnp.zeros((heads_local, query_count, head_size), jnp.float32),
    )

    def visit(block, state):
        first_slot = block * block_width
        block_keys = lax.dynamic_slice_in_dim(beacon_keys, first_slot, block_width, 1)
        block_values = lax.dynamic_slice_in_dim(beacon_values, first_slot, block_width, 1)
        slot_index = first_slot + jnp.arange(block_width, dtype=jnp.int32)
        owner = slot_index // slots_dev
        in_range = (owner >= low_rank) & (owner < high_rank)
        earlier = (slot_index // BEACONS)[None, :] < query_span[:, None]
        allowed = (in_range[None, :] & earlier)[None]
        return combine_partials(state, partial_attend(queries, block_keys, block_values, allowed))

    first_block = low_rank // group
    last_block = (high_rank + group - 1) // group
    return lax.fori_loop(first_block, last_block, visit, start_state)


def on_device_general(tokens_in, tempo_ids, tempo_table, w_query, w_key, w_value):
    row_count = tokens_in.shape[0]
    col_width = w_query.shape[1]
    heads_local = col_width // HEAD_DIM
    ctx_count = lax.axis_size("ctx")
    ctx_rank = lax.axis_index("ctx")
    spans_dev = row_count // SPAN
    slots_dev = spans_dev * BEACONS
    target = max(1, 256 // slots_dev)
    group = min(ctx_count, 1 << target.bit_length() - 1)
    selector = (
        tempo_ids[:, None] == jnp.arange(tempo_table.shape[0], dtype=jnp.int32)[None, :]
    ).astype(jnp.bfloat16)
    hidden = (
        tokens_in.astype(jnp.float32)
        + jnp.dot(selector, tempo_table, preferred_element_type=jnp.float32)
    ).astype(jnp.bfloat16)
    pieces = (
        lax.all_gather(w_query, "ctx", axis=0, tiled=True),
        lax.all_gather(w_key, "ctx", axis=0, tiled=True),
        lax.all_gather(w_value, "ctx", axis=0, tiled=True),
    )
    projected = tuple(
        (jnp.dot(hidden, piece, preferred_element_type=jnp.float32) for piece in pieces)
    )
    queries = projected[0].astype(jnp.bfloat16)
    keys = projected[1].astype(jnp.bfloat16)
    values = projected[2].astype(jnp.bfloat16)
    pool_scale = POOL ** (-0.5)
    own_keys = (
        jnp.sum(keys.reshape(slots_dev, POOL, col_width).astype(jnp.float32), axis=1) * pool_scale
    ).astype(jnp.bfloat16)
    own_values = (
        jnp.sum(values.reshape(slots_dev, POOL, col_width).astype(jnp.float32), axis=1) * pool_scale
    ).astype(jnp.bfloat16)
    every_keys, every_values = (
        lax.all_gather(own_keys, "ctx", axis=0, tiled=True),
        lax.all_gather(own_values, "ctx", axis=0, tiled=True),
    )
    beacon_keys = by_heads(every_keys, heads_local)
    beacon_values = by_heads(every_values, heads_local)
    query_heads = by_heads(queries, heads_local)
    local_span = jnp.arange(row_count, dtype=jnp.int32) // SPAN
    own_span = ctx_rank * spans_dev + local_span

    def fold_spans(matrix):
        return by_heads(matrix, heads_local)

    causal = (
        jnp.arange(SPAN, dtype=jnp.int32)[:, None] >= jnp.arange(SPAN, dtype=jnp.int32)[None, :]
    )[None]
    inside = partial_attend(fold_spans(queries), fold_spans(keys), fold_spans(values), causal)
    inside = (inside[0], inside[1], inside[2])
    upper_rank = ctx_rank + 1
    remote = beacon_partial(
        query_heads,
        own_span,
        beacon_keys,
        beacon_values,
        jnp.zeros((), jnp.int32),
        upper_rank,
        group,
        slots_dev,
    )
    _, totals, summed = combine_partials(inside, remote)
    attended = summed / totals[..., None]
    return attended.transpose(1, 0, 2).reshape(row_count, col_width).astype(jnp.bfloat16)


VMEM = pl.BlockSpec(memory_space=pltpu.VMEM)
HBM = pl.BlockSpec(memory_space=pltpu.HBM)


def spots():
    rank = lax.axis_index("ctx")
    return (rank, rank ^ 1, rank ^ 2, rank ^ 3, lax.axis_index("groups"))


def in_hbm(array):
    return pltpu.with_memory_space_constraint(array, pltpu.HBM)


def mm(a, b):
    return jnp.dot(a, b, preferred_element_type=jnp.float32)


def cost(flops, moved, exps=0):
    return pl.CostEstimate(flops=flops, bytes_accessed=moved, transcendentals=exps)


def limit(mebibytes):
    return pltpu.CompilerParams(vmem_limit_bytes=mebibytes << 20)


def span_of(index, size):
    return pl.ds(pl.multiple_of(index * size, size), size)


def run_copies(copies):
    for copy in copies:
        copy.start()
    for copy in copies:
        copy.wait()


def cut_kernel(*refs):
    s_ref = spots()
    count = len(refs) // 2
    sems = refs[-1]
    piece, half = refs[count].shape
    step = piece // 2
    cols = span_of(lax.rem(s_ref[0], 2), half)
    copies = []
    for source, target in zip(refs[:count], refs[count:-1]):
        for low in range(0, piece, step):
            rows = pl.ds(pl.multiple_of(s_ref[4] * piece + low, step), step)
            copies.append(
                pltpu.make_async_copy(
                    source.at[rows, cols], target.at[pl.ds(low, step)], sems.at[len(copies)]
                )
            )
    run_copies(copies)


def cut_same(*weights):
    depth, width = weights[0].shape
    count = len(weights)
    shape = jax.ShapeDtypeStruct((depth // 2, width // 2), jnp.bfloat16)
    return pl.pallas_call(
        cut_kernel,
        in_specs=[HBM] * count,
        out_specs=[VMEM] * count,
        out_shape=[shape] * count,
        scratch_shapes=[pltpu.SemaphoreType.DMA((2 * count,))],
        compiler_params=limit(1),
        cost_estimate=cost(0, count * depth * width),
        name="cut_same",
    )(*[in_hbm(w) for w in weights])


def prepare_kernel(
    ids_hbm,
    tokens_ref,
    table_hbm,
    wk_ref,
    wv_ref,
    wq_ref,
    hidden_ref,
    own_ref,
    k_here_ref,
    v_here_ref,
    there_ref,
    q_ref,
    ids_ref,
    table_ref,
    sems,
    small_sems,
    cut_sems,
):
    s_ref = spots()
    buckets, width = table_ref.shape
    rows = tokens_ref.shape[0]
    piece, half = k_here_ref.shape
    tile = TILE // 2
    step = min(width, 512)
    ahead = 4
    core = lax.rem(s_ref[0], 2)
    mine, other = span_of(core, half), span_of(1 - core, half)
    here, there = span_of(s_ref[4], piece), span_of(1 - s_ref[4], piece)
    pairs = (
        (wk_ref.at[here, other], k_here_ref),
        (wv_ref.at[here, other], v_here_ref),
        (wk_ref.at[there, other], there_ref.at[0]),
        (wv_ref.at[there, other], there_ref.at[1]),
        (wq_ref.at[:, other], q_ref),
        (wk_ref.at[:, mine], own_ref.at[0]),
        (wv_ref.at[:, mine], own_ref.at[1]),
        (wq_ref.at[:, mine], own_ref.at[2]),
    )
    cuts = [
        pltpu.make_async_copy(source, target, cut_sems.at[i])
        for i, (source, target) in enumerate(pairs)
    ]
    copies = [
        pltpu.make_async_copy(
            tokens_ref.at[pl.ds(i * tile, tile)], hidden_ref.at[pl.ds(i * tile, tile)], sems.at[i]
        )
        for i in range(rows // tile)
    ]
    small = [
        pltpu.make_async_copy(ids_hbm, ids_ref, small_sems.at[0]),
        pltpu.make_async_copy(table_hbm, table_ref, small_sems.at[1]),
    ]
    for copy in small + copies[:ahead]:
        copy.start()
    for copy in small:
        copy.wait()
    for i, copy in enumerate(copies):
        part = slice(i * tile, (i + 1) * tile)
        bucket = lax.broadcasted_iota(jnp.int32, (buckets, tile), 0)
        picked = jnp.where(bucket == ids_ref[:, part], 1.0, 0.0).astype(jnp.bfloat16)
        copy.wait()
        if i + ahead < len(copies):
            copies[i + ahead].start()
        for cut in cuts[2 * i : 2 * i + 2]:
            cut.start()
        for col in range(0, width, step):
            cols = slice(col, col + step)
            tempo = lax.dot_general(
                picked,
                table_ref[:, cols],
                (((0,), (0,)), ((), ())),
                preferred_element_type=jnp.float32,
            )
            tokens = hidden_ref[part, cols].astype(jnp.float32)
            hidden_ref[part, cols] = (tokens + tempo).astype(hidden_ref.dtype)
    for cut in cuts:
        cut.wait()


def prepare(tokens_in, tempo_ids, tempo_table, weights):
    rows, width = tokens_in.shape
    depth, full = weights[0].shape
    piece, half = depth // 2, full // 2
    shapes = (
        (rows, width),
        (3, depth, half),
        (piece, half),
        (piece, half),
        (2, piece, half),
        (depth, half),
    )
    return pl.pallas_call(
        prepare_kernel,
        in_specs=[HBM] * 6,
        out_specs=[VMEM] * 6,
        out_shape=[jax.ShapeDtypeStruct(shape, jnp.bfloat16) for shape in shapes],
        scratch_shapes=[
            pltpu.VMEM((1, rows), jnp.int32),
            pltpu.VMEM(tempo_table.shape, jnp.bfloat16),
            pltpu.SemaphoreType.DMA((2 * rows // TILE,)),
            pltpu.SemaphoreType.DMA((2,)),
            pltpu.SemaphoreType.DMA((8,)),
        ],
        compiler_params=limit(4),
        cost_estimate=cost(2 * rows * 256 * width, 4 * rows * width),
        name="prepare",
    )(
        in_hbm(tempo_ids.reshape(1, rows)),
        in_hbm(tokens_in),
        in_hbm(tempo_table),
        *[in_hbm(w) for w in weights],
    )


def local_kernel(
    hidden_ref,
    own_ref,
    k_here_ref,
    v_here_ref,
    there_ref,
    q_ref,
    kv_sum_ref,
    q_sum_ref,
    *q_parts,
):
    s_ref = spots()
    rows = hidden_ref.shape[0]
    piece, half = k_here_ref.shape
    own, mate, song = s_ref[0], s_ref[1], s_ref[4]
    first = 0
    for out_ref in q_parts:
        out_ref[...] = q_ref[first : first + out_ref.shape[0], :]
        first += out_ref.shape[0]
    for low in range(0, rows, TILE):
        part = slice(low, low + TILE)
        mine = hidden_ref[part, span_of(own, 2 * piece)]
        here = hidden_ref[part, span_of(2 * mate + song, piece)]
        there = hidden_ref[part, span_of(2 * mate + 1 - song, piece)]
        for place, here_ref in enumerate((k_here_ref, v_here_ref)):
            kv_sum_ref[part, place * half : (place + 1) * half] = (
                mm(mine, own_ref[place]) + mm(here, here_ref[...]) + mm(there, there_ref[place])
            )
        other = hidden_ref[part, span_of(mate, 2 * piece)]
        q_sum_ref[part, :] = mm(mine, own_ref[2]) + mm(other, q_ref[...])


def local_part(hidden, own_weights, mate_weights, parts):
    rows = hidden.shape[0]
    _, depth, half = own_weights.shape
    return pl.pallas_call(
        local_kernel,
        in_specs=[VMEM] * 6,
        out_specs=[VMEM] * (2 + len(parts)),
        out_shape=[
            jax.ShapeDtypeStruct((rows, 2 * half), jnp.float32),
            jax.ShapeDtypeStruct((rows, half), jnp.float32),
        ]
        + [jax.ShapeDtypeStruct((count, half), jnp.bfloat16) for count in parts],
        compiler_params=limit(6),
        cost_estimate=cost(12 * rows * depth * half, 4 * rows * depth + 12 * rows * half),
        name="local_part",
    )(hidden, own_weights, *mate_weights)


def pool_rows(rounded):
    rows, half = rounded.shape
    groups = rounded.astype(jnp.float32).reshape(rows // POOL, POOL, half)
    return (jnp.sum(groups, axis=1) * POOL ** (-0.5)).astype(jnp.bfloat16)


def early_kernel(
    own_ref,
    mate_ref,
    own_sum,
    mate_sum,
    k_mine,
    v_mine,
    k_twin,
    v_twin,
    k_far,
    v_far,
    out_ref,
):
    s_ref = spots()
    rows = own_ref.shape[0]
    piece, half = k_mine.shape
    same, cross, song = s_ref[2], s_ref[3], s_ref[4]
    weights = ((k_mine, k_twin, k_far), (v_mine, v_twin, v_far))
    for turn, (h_ref, sum_ref) in enumerate(((own_ref, own_sum), (mate_ref, mate_sum))):
        for low in range(0, rows, TILE):
            part = slice(low, low + TILE)
            target = slice(turn * rows + low, turn * rows + low + TILE)
            mine = h_ref[part, span_of(2 * same + song, piece)]
            twin = h_ref[part, span_of(2 * same + 1 - song, piece)]
            far = h_ref[part, span_of(2 * cross + song, piece)]
            for place, (w_mine, w_twin, w_far) in enumerate(weights):
                cols = slice(place * half, (place + 1) * half)
                out_ref[target, cols] = (
                    sum_ref[part, cols]
                    + mm(mine, w_mine[...])
                    + mm(twin, w_twin[...])
                    + mm(far, w_far[...])
                )


def early_sums(own, mate, sums, pieces):
    rows = own.shape[0]
    piece, half = pieces[0].shape
    return pl.pallas_call(
        early_kernel,
        in_specs=[VMEM] * 10,
        out_specs=VMEM,
        out_shape=jax.ShapeDtypeStruct((2 * rows, 2 * half), jnp.float32),
        compiler_params=limit(6),
        cost_estimate=cost(24 * rows * piece * half, 12 * rows * piece + 32 * rows * half),
        name="early_sums",
    )(own, mate, *sums, *pieces)


def late_kernel(
    own_ref, mate_ref, sum_ref, k_twin, v_twin, keys_ref, values_ref, near_ref
):
    s_ref = spots()
    rows = own_ref.shape[0]
    piece, half = k_twin.shape
    column = 2 * s_ref[3] + 1 - s_ref[4]
    for turn, h_ref in enumerate((own_ref, mate_ref)):
        for low in range(0, rows, TILE):
            hidden = h_ref[low : low + TILE, span_of(column, piece)]
            start = turn * rows + low
            target = slice(start, start + TILE)
            slots = slice(start // POOL, (start + TILE) // POOL)
            for place, (w_ref, out_ref) in enumerate(((k_twin, keys_ref), (v_twin, values_ref))):
                cols = slice(place * half, (place + 1) * half)
                rounded = (sum_ref[target, cols] + mm(hidden, w_ref[...])).astype(jnp.bfloat16)
                out_ref[target, :] = rounded
                near_ref[place, slots, :] = pool_rows(rounded)


def late_keys_values(own, mate, sums, k_twin, v_twin):
    rows = own.shape[0]
    piece, half = k_twin.shape
    return pl.pallas_call(
        late_kernel,
        in_specs=[VMEM] * 5,
        out_specs=[VMEM] * 3,
        out_shape=[
            jax.ShapeDtypeStruct((2 * rows, half), jnp.bfloat16),
            jax.ShapeDtypeStruct((2 * rows, half), jnp.bfloat16),
            jax.ShapeDtypeStruct((2, 2 * rows // POOL, half), jnp.bfloat16),
        ],
        compiler_params=limit(6),
        cost_estimate=cost(8 * rows * piece * half, 4 * rows * piece + 24 * rows * half),
        name="late_keys_values",
    )(own, mate, sums, k_twin, v_twin)


def query_kernel(columns, own_ref, mate_ref, *refs):
    s_ref = spots()
    rows = own_ref.shape[0]
    sums, weights, out_ref = refs[: -1 - len(columns)], refs[-1 - len(columns) : -1], refs[-1]
    for turn, h_ref in enumerate((own_ref, mate_ref)):
        for low in range(0, rows, TILE):
            target = slice(turn * rows + low, turn * rows + low + TILE)
            if len(sums) == 2:
                total = sums[turn][low : low + TILE, :]
            else:
                total = sums[0][target, :]
            for column, w_ref in zip(columns, weights):
                cols = pl.ds(pl.multiple_of(column(s_ref), TILE), w_ref.shape[0])
                total += mm(h_ref[low : low + TILE, cols], w_ref[...])
            out_ref[target, :] = total.astype(out_ref.dtype)


def query_sums(own, mate, sums, columns, pieces, dtype):
    rows = own.shape[0]
    half = pieces[0].shape[1]
    deep = sum(piece.shape[0] for piece in pieces)
    return pl.pallas_call(
        functools.partial(query_kernel, columns),
        in_specs=[VMEM] * (2 + len(sums) + len(pieces)),
        out_specs=VMEM,
        out_shape=jax.ShapeDtypeStruct((2 * rows, half), dtype),
        compiler_params=limit(6),
        cost_estimate=cost(4 * rows * deep * half, 4 * rows * deep + 16 * rows * half),
    )(own, mate, *sums, *pieces)


def attend_rows(
    turn, bounds, s_ref, queries_ref, keys_ref, values_ref, near_ref, far_ref, store
):
    base = turn * SPAN
    span = s_ref[turn]
    factor = HEAD_DIM ** (-0.5) * LOG2_E
    contract = (((1,), (1,)), ((), ()))
    slots = near_ref.shape[1] + far_ref.shape[1]
    owner = lax.broadcasted_iota(jnp.int32, (1, slots), 1) // BEACONS
    allowed = jnp.zeros((1, slots), jnp.int32)
    for place in range(slots // BEACONS):
        visible = (s_ref[place] < span).astype(jnp.int32)
        allowed = jnp.where(owner == place, visible, allowed)
    allowed = allowed > 0
    causal = lax.broadcasted_iota(jnp.int32, (TILE, TILE), 0) >= lax.broadcasted_iota(
        jnp.int32, (TILE, TILE), 1
    )
    start, stop = bounds
    tiles = range(start, stop, TILE)
    blocks = range(0, stop, TILE)
    heads = range(queries_ref.shape[1] // HEAD_DIM)

    def dots(query, keys):
        return lax.dot_general(query, keys, contract, preferred_element_type=jnp.float32)

    def scores(head):
        cols = slice(head * HEAD_DIM, (head + 1) * HEAD_DIM)
        query = queries_ref[base + start : base + stop, cols]
        beacon_keys = jnp.concatenate([near_ref[0, :, cols], far_ref[0, :, cols]], axis=0)
        beacon_score = dots(query, beacon_keys)
        inside = [
            dots(query[max(first - start, 0) :], keys_ref[base + first : base + first + TILE, cols])
            for first in blocks
        ]
        return beacon_score, inside

    def finish(head, beacon_score, inside):
        cols = slice(head * HEAD_DIM, (head + 1) * HEAD_DIM)
        amounts, beacon_weights, weights = [], [], [[] for _ in blocks]
        for low in tiles:
            row = low - start
            parts = [jnp.where(allowed, beacon_score[row : row + TILE], LOWEST)]
            for first in range(0, low + TILE, TILE):
                row = low - max(first, start)
                part = inside[first // TILE][row : row + TILE]
                parts.append(jnp.where(causal, part, LOWEST) if first == low else part)
            score = jnp.concatenate(parts, axis=1)
            highest = jnp.max(score, axis=1, keepdims=True)
            weight = jnp.exp2((score - highest) * factor)
            amounts.append(jnp.sum(weight, axis=1, keepdims=True))
            rounded = weight.astype(jnp.bfloat16)
            beacon_weights.append(rounded[:, :slots])
            for first in range(0, low + TILE, TILE):
                weights[first // TILE].append(rounded[:, slots + first : slots + first + TILE])
        beacon_values = jnp.concatenate([near_ref[1, :, cols], far_ref[1, :, cols]], axis=0)
        summed = mm(jnp.concatenate(beacon_weights, axis=0), beacon_values)
        summed = [summed[i * TILE : (i + 1) * TILE] for i in range(len(tiles))]
        for first, group in zip(blocks, weights):
            term = mm(
                jnp.concatenate(group, axis=0), values_ref[base + first : base + first + TILE, cols]
            )
            skip = len(tiles) - len(group)
            for i in range(len(group)):
                summed[skip + i] += term[i * TILE : (i + 1) * TILE]
        for low, value, amount in zip(tiles, summed, amounts):
            store(low - start, cols, value / amount)

    pending = None
    for head in heads:
        score = scores(head)
        if pending is not None:
            finish(*pending)
        pending = (head, *score)
    finish(*pending)


def attend_first_kernel(turn, bounds, *refs):
    s_ref = spots()
    out_ref = refs[-1]

    def store(row, cols, value):
        out_ref[row : row + TILE, cols] = value.astype(out_ref.dtype)

    attend_rows(turn, bounds, s_ref, *refs[:-1], store)


def attend_last_kernel(bounds, part_ref, from_mate_ref, *refs):
    s_ref = spots()
    out_ref, scratch, sems = refs[-3:]
    start, stop = bounds
    half = scratch.shape[1]
    core = lax.rem(s_ref[0], 2)
    mine, other = span_of(core, half), span_of(1 - core, half)
    rows = from_mate_ref.shape[0]
    middle = rows // 2
    copies = [
        pltpu.make_async_copy(part_ref, out_ref.at[pl.ds(stop, rows - stop), mine], sems.at[0]),
    ] + [
        pltpu.make_async_copy(
            from_mate_ref.at[pl.ds(low, middle)],
            out_ref.at[pl.ds(low, middle), other],
            sems.at[1 + low // middle],
        )
        for low in (0, middle)
    ]
    for copy in copies:
        copy.start()

    def store(row, cols, value):
        scratch[row : row + TILE, cols] = value.astype(scratch.dtype)
        if cols.stop == half:
            copy = pltpu.make_async_copy(
                scratch.at[pl.ds(row, TILE)],
                out_ref.at[pl.ds(start + row, TILE), mine],
                sems.at[3 + row // TILE],
            )
            copy.start()
            copies.append(copy)

    attend_rows(0, bounds, s_ref, *refs[:-3], store)
    for copy in copies:
        copy.wait()


def attend(kernel, bounds, arrays, out_spec, shape, scratch=()):
    width = shape[1]
    area = (bounds[1] - bounds[0]) * bounds[1]
    return pl.pallas_call(
        kernel,
        in_specs=[VMEM] * len(arrays),
        out_specs=out_spec,
        out_shape=jax.ShapeDtypeStruct(shape, jnp.bfloat16),
        scratch_shapes=list(scratch),
        compiler_params=limit(12),
        cost_estimate=cost(4 * area * width, 8 * shape[0] * width, area * width // HEAD_DIM),
    )(*arrays)


def on_device(tokens_in, tempo_ids, tempo_table, w_query, w_key, w_value):
    depth, width = w_key.shape
    rows = tokens_in.shape[0]
    half = width // 2
    piece = depth // 2
    ranks = range(lax.axis_size("ctx"))
    weights = (w_key, w_value, w_query)

    def to_mate(array):
        return lax.ppermute(array, "ctx", [(r, r ^ 1) for r in ranks])

    def to_far(array):
        return lax.ppermute(array, "ctx", [(r, r ^ 2) for r in ranks])

    def to_twin(array):
        return lax.ppermute(array, "groups", [(0, 1), (1, 0)])

    k_cut, v_cut, q_cut = cut_same(*weights)
    own, own_weights, *cuts = prepare(tokens_in, tempo_ids, tempo_table, weights)
    k_mine = to_far(k_cut)
    v_mine = to_far(v_cut)
    q_mine = to_far(q_cut)
    mate_k = to_mate(cuts[0])
    mate_v = to_mate(cuts[1])
    mate_there = to_mate(cuts[2])
    mate_q = to_mate(cuts[3])
    mate = to_mate(own)
    k_far_mine = to_far(mate_k)
    v_far_mine = to_far(mate_v)
    k_twin = to_twin(k_mine)
    v_twin = to_twin(v_mine)
    k_far_twin = to_twin(k_far_mine)
    v_far_twin = to_twin(v_far_mine)
    q_same_twin = to_twin(q_mine)

    mate_weights = (mate_k, mate_v, mate_there, mate_q)
    parts = (depth - depth // 4, depth // 4)
    own_kv, own_q, *q_parts = local_part(own, own_weights, mate_weights, parts)
    q_cross0 = to_far(q_parts[0])
    q_cross1 = to_far(q_parts[1])
    mate_kv, mate_q_sum = local_part(mate, own_weights, mate_weights, ())
    pieces = (k_mine, v_mine, k_twin, v_twin, k_far_mine, v_far_mine)
    kv_sums = early_sums(own, mate, (own_kv, mate_kv), pieces)
    keys, values, near = late_keys_values(
        own, mate, kv_sums, k_far_twin, v_far_twin
    )
    far = to_far(near)

    def add_queries(sums, parts, dtype):
        columns, pieces = zip(*parts)
        return query_sums(own, mate, sums, columns, pieces, dtype)

    same_mine = (lambda s: (2 * s[2] + s[4]) * piece, q_mine)
    same_twin = (lambda s: (2 * s[2] + 1 - s[4]) * piece, q_same_twin)
    cross = [
        (lambda s: s[3] * depth, q_cross0),
        (lambda s: s[3] * depth + parts[0], q_cross1),
    ]
    q_sums = add_queries((own_q, mate_q_sum), (same_mine, cross[0]), jnp.float32)
    q_sums = add_queries((q_sums,), (same_twin,), jnp.float32)
    queries = add_queries((q_sums,), (cross[1],), jnp.bfloat16)
    rest = (queries, keys, values, near, far)
    later = (TILE, rows)
    kernel = functools.partial(attend_first_kernel, 1, (0, rows))
    arrays = rest
    for_mate = attend(kernel, (0, rows), arrays, VMEM, (rows, half))
    from_mate = to_mate(for_mate)
    kernel = functools.partial(attend_first_kernel, 0, later)
    arrays = rest
    part = attend(kernel, later, arrays, VMEM, (rows - TILE, half))
    scratch = (
        pltpu.VMEM((TILE, half), jnp.bfloat16),
        pltpu.SemaphoreType.DMA((4,)),
    )
    bounds = (0, TILE)
    kernel = functools.partial(attend_last_kernel, bounds)
    arrays = (part, from_mate, *rest)
    return attend(kernel, bounds, arrays, HBM, (rows, width), scratch)


def fits(mesh):
    return mesh.shape["ctx"] == 4 and mesh.shape["groups"] == 2


def solution(mesh):
    in_specs = (
        P(("groups", "ctx"), None),
        P(("groups", "ctx")),
        P(),
        P("ctx", "head"),
        P("ctx", "head"),
        P("ctx", "head"),
    )
    out_specs = P(("groups", "ctx"), "head")

    planned = fits(mesh)

    def body(*arrays):
        return (on_device if planned else on_device_general)(*arrays)

    return jax.shard_map(
        body, mesh=mesh, in_specs=in_specs, out_specs=out_specs, check_vma=False
    )
```
